32 devices in a mesh: segment: 4 (over z), dp: 8 (over y, x, core).
Axes of the slice: x: 2, y: 2, z: 4, core: 2. Of those that a mesh axis runs over, the one named last changes fastest.
Arguments:
- acts: bfloat16 [4, 1024, 8192], P('segment', 'dp'), may hold values from -6 to 6
- weights: bfloat16 [4, 2, 64, 128, 128], P('segment'), may hold values from -0.5 to 0.5
- gains: float32 [4, 8192], P('segment'), may hold values from 0.5 to 1.5
- cotangent: bfloat16 [1024, 8192], P('dp'), may hold values from -6 to 6
- block_order: int32 [64], replicated, may hold values from 0 to 63, each once
- owner_table: int32 [128], replicated, may hold values from 0 to 127, each once
Outputs:
- input_grads: bfloat16 [4, 1024, 8192], P('segment', 'dp')
- block_grads: float32 [4, 128, 128, 128], P('segment', 'dp')
- gain_grads: float32 [4, 8192], P('segment', 'dp')
The draws below stay inside these ranges and needn't reach their ends.
Inputs may be any that keep to these rules, and one draw needn't show every extreme that they name: `block_order`: a permutation. `owner_table`: a permutation.
All inputs are finite; a program needn't handle non-finite values.
Results may differ from the reference program's by a relative error of at most 0.012.
Values may be sent and summed in bfloat16 or wider, within the bound.
No kernel may reach another device: no remote copies, remote signals or barrier semaphores. Data moves between devices by JAX's collectives and lax.ppermute only.
A program may use at most 128 MiB of HBM per device.

```python
import jax
import jax.numpy as jnp
from jax import lax

FACTOR_BLOCKS = 64
BLOCK_EXTENT = 128
D = 8192
TOKENS = 1024
LAYERS = 4
N_SEGMENT = 4


def raised(entries, rng, source, target, shards_of, factor):
    owner, partner = [(jnp.arange(entries.shape[dim]) // (entries.shape[dim] // shards_of)).reshape([-1 if axis == dim else 1 for axis in range(entries.ndim)]) for dim in (source, target)]
    chosen = jax.random.permutation(rng, shards_of)[partner]
    strong = (owner == chosen) | (owner == (partner + shards_of // 2) % shards_of)
    return jnp.where(strong, factor * entries, entries)


def level_of(own_key, dims, shards, low, largest):
    gain = 1.0
    for dim, blocks in shards:
        heights = jax.random.uniform(jax.random.fold_in(jax.random.fold_in(own_key, 6), dim), (blocks,), jnp.float32, low / len(shards), largest / len(shards))
        gain = gain * jnp.repeat(jnp.exp(heights), dims[dim] // blocks).reshape((-1,) + (1,) * (len(dims) - 1 - dim))
    return gain


def normal_values(stream_key, shape, scale, reach, split=(), kind=jnp.bfloat16):
    gain = level_of(stream_key, shape, split, -0.22, 0.18) if split else 1.0
    array = jax.random.normal(stream_key, shape, jnp.float32) * scale * gain
    return jnp.minimum(jnp.maximum(array, -reach), reach).astype(kind)


def gaussian_with(own_key, extent, width, limit, pieces, heavy, held_as=jnp.bfloat16):
    entries = width * jax.random.normal(own_key, extent, jnp.float32)
    if pieces:
        entries = entries * level_of(own_key, extent, pieces, -0.22, 0.18)
    return jnp.clip(raised(entries, jax.random.fold_in(own_key, 3), *heavy), -limit, limit).astype(held_as)


def setup_inputs(seed: int = 0) -> dict:
    streams_of = jax.random.split(jax.random.key(seed), 7)
    return {
        "acts": normal_values(streams_of[0], (LAYERS, TOKENS, D), 1.0, 6.0, ((0, 4), (1, 8))),
        "weights": normal_values(streams_of[1], (LAYERS, 2, FACTOR_BLOCKS, BLOCK_EXTENT, BLOCK_EXTENT), BLOCK_EXTENT ** -0.5, 0.5, ((0, 4),)),
        "gains": jnp.clip(1.0 + 0.1 * jax.random.normal(streams_of[2], (LAYERS, D), jnp.float32), 0.5, 1.5),
        "cotangent": gaussian_with(streams_of[3], (TOKENS, D), 1.0, 6.0, ((0, 8),), (0, 1, 8, 2.0)),
        "block_order": jax.random.permutation(streams_of[4], FACTOR_BLOCKS).astype(jnp.int32),
        "owner_table": jax.random.permutation(streams_of[5], 2 * FACTOR_BLOCKS).astype(jnp.int32),
    }


epsilon = 1e-05

def gelu_pair(value_rows):
    cdf = 0.5 * (1.0 + lax.erf(value_rows * 0.7071067811865476))
    density = jnp.exp(-0.5 * value_rows * value_rows) * 0.3989422804014327
    return (value_rows * cdf, cdf + value_rows * density)

def layer_back(inputs, layer_weights, norm_gain, output_gradient, order, inverse):
    element_count = inputs.shape[0]
    first = layer_weights[0].astype(jnp.float32)
    second = layer_weights[1].astype(jnp.float32)
    value_rows = inputs.astype(jnp.float32)
    monarch_factor = lax.rsqrt(lax.optimization_barrier(jnp.mean(value_rows * value_rows, axis=-1, keepdims=True)) + epsilon)
    centered_input = value_rows * monarch_factor
    normalized_rows = (centered_input * norm_gain).astype(jnp.bfloat16).reshape(element_count, FACTOR_BLOCKS, BLOCK_EXTENT)
    pre_act = jnp.einsum('tjk,jkl->tjl', normalized_rows.astype(jnp.float32), first)
    activ, slope = gelu_pair(pre_act)
    activ = activ.astype(jnp.bfloat16)
    mixed_in = jnp.take(activ.transpose(0, 2, 1).reshape(element_count, FACTOR_BLOCKS, BLOCK_EXTENT), order, axis=1)
    grad_blocks = output_gradient.reshape(element_count, FACTOR_BLOCKS, BLOCK_EXTENT)
    grad_mixed = jnp.einsum('tjl,jkl->tjk', grad_blocks.astype(jnp.float32), second)
    grad_act = jnp.take(grad_mixed, inverse, axis=1).reshape(element_count, BLOCK_EXTENT, FACTOR_BLOCKS).transpose(0, 2, 1)
    grad_pre = (grad_act * slope).astype(jnp.bfloat16)
    normalized_gradient = jnp.einsum('tjl,jkl->tjk', grad_pre.astype(jnp.float32), first).reshape(element_count, FACTOR_BLOCKS * BLOCK_EXTENT)
    gain_portion = lax.optimization_barrier(jnp.sum(normalized_gradient * centered_input, axis=0))
    centered_gradient = normalized_gradient * norm_gain
    inner_product = lax.optimization_barrier(jnp.mean(centered_gradient * centered_input, axis=-1, keepdims=True))
    input_gradient = (output_gradient.astype(jnp.float32) + monarch_factor * (centered_gradient - centered_input * inner_product)).astype(jnp.bfloat16)
    first_grad = jnp.einsum('tjk,tjl->jkl', normalized_rows.astype(jnp.float32), grad_pre.astype(jnp.float32))
    second_grad = jnp.einsum('tjk,tjl->jkl', mixed_in.astype(jnp.float32), grad_blocks.astype(jnp.float32))
    return (input_gradient, first_grad, second_grad, gain_portion)

def reference(acts, weights, gains, cotangent, block_order, owner_table):
    inverse = jnp.argsort(block_order).astype(jnp.int32)
    scale = 1.0 / float(TOKENS) ** 0.5
    current = cotangent
    grads_in = [None] * N_SEGMENT
    grads_blocks = [None] * N_SEGMENT
    grads_gain = [None] * N_SEGMENT
    for layer in reversed(range(N_SEGMENT)):
        input_gradient, first_grad, second_grad, gain_portion = layer_back(acts[layer], weights[layer], gains[layer], current, block_order, inverse)
        stacked = jnp.concatenate([first_grad, second_grad], axis=0)
        grads_in[layer] = input_gradient
        grads_blocks[layer] = jnp.take(stacked, owner_table, axis=0) * scale
        grads_gain[layer] = gain_portion * scale
        current = input_gradient
    return (jnp.stack(grads_in), jnp.stack(grads_blocks), jnp.stack(grads_gain))
```

```python
import functools
import math

import jax
import jax.numpy as jnp
from jax import lax
from jax.experimental import pallas as pl
from jax.experimental.pallas import tpu as pltpu
from jax.sharding import PartitionSpec as P

F = 64
B = 128
EPS = 1e-05
CHUNKS = 8
LAG = 2
ANY = pl.BlockSpec(memory_space=pl.ANY)
VMEM = pl.BlockSpec(memory_space=pltpu.VMEM)
SMEM = pl.BlockSpec(memory_space=pltpu.SMEM)
NT = (((1,), (1,)), ((), ()))


def dot(a, b):
    return jnp.dot(a, b, preferred_element_type=jnp.float32)


def dot_nt(a, b):
    return lax.dot_general(a, b, NT, preferred_element_type=jnp.float32)


def col(j):
    if isinstance(j, int):
        return pl.ds(j * B, B)
    return pl.ds(pl.multiple_of(j * B, B), B)


def exchange(parts, lane_bit):
    lane = lax.broadcasted_iota(jnp.int32, parts[0].shape, 1)
    parts = list(parts)
    for i in range(3):
        shift = 1 << (lane_bit + i)
        upper = (lane & shift) != 0
        for low in range(8):
            if low & (1 << i):
                continue
            high = low | (1 << i)
            a, b = parts[low], parts[high]
            parts[low] = jnp.where(upper, pltpu.roll(b, shift, 1), a)
            parts[high] = jnp.where(upper, b, pltpu.roll(a, B - shift, 1))
    return parts


def gelu_pair(v):
    cdf = 0.5 * (1.0 + lax.erf(v * 0.7071067811865476))
    density = jnp.exp(-0.5 * v * v) * 0.3989422804014327
    return v * cdf, cdf + v * density


def inverse_rms(x_ref, rows):
    def add(j, total):
        v = x_ref[rows, col(j)].astype(jnp.float32)
        return total + v * v

    size = x_ref.shape[0] if rows == slice(None) else rows.size
    total = lax.fori_loop(0, F, add, jnp.zeros((size, B), jnp.float32), unroll=8)
    mean = jnp.sum(total, axis=1, keepdims=True) * (1.0 / (F * B))
    return lax.rsqrt(mean + EPS)


def prologue_kernel(order_ref, x_ref, gain_ref, w0_ref, eye_ref, take_ref, slope_ref, left_ref, inv_ref, half_ref, mix_ref):
    step = pl.program_id(0)
    n = x_ref.shape[0]
    sub = 32

    @pl.when(step == 0)
    def _():
        inv_ref[...] = jnp.broadcast_to(inverse_rms(x_ref, slice(None)), (n, B))

    eye = eye_ref[...]
    base = step * 8
    for i in range(8):
        at = col(base + i)
        h = (x_ref[:, at].astype(jnp.float32) * inv_ref[...] * gain_ref[:, at]).astype(jnp.bfloat16)
        left_ref[base + i] = dot_nt(eye, h).astype(jnp.bfloat16)
        z, slope = gelu_pair(dot(h, w0_ref[i]))
        slope_ref[:, col(i)] = slope.astype(slope_ref.dtype)
        half_ref[base + i] = z
    for t in range(0, n, sub):
        rows = pl.ds(t, sub)
        parts = exchange([half_ref[base + i, rows, :] for i in range(8)], 1)
        for i in range(8):
            half_ref[base + i, rows, :] = parts[i]

    @pl.when(step == pl.num_programs(0) - 1)
    def _():
        for low in range(8):
            for t in range(0, n, sub):
                rows = pl.ds(t, sub)
                parts = exchange([half_ref[8 * g + low, rows, :] for g in range(8)], 4)
                for g in range(8):
                    mix_ref[8 * g + low, rows, :] = parts[g].astype(jnp.bfloat16)
        take = take_ref[...]

        @pl.loop(0, F)
        def _(j):
            left_ref[F + j] = dot_nt(take, mix_ref[order_ref[j]]).astype(jnp.bfloat16)


def prologue(order, x, gain, w0, eye, take):
    n = x.shape[0]
    whole = lambda *shape: pl.BlockSpec(shape, lambda s: (0,) * len(shape))
    return pl.pallas_call(
        prologue_kernel,
        grid=(F // 8,),
        out_shape=(
            jax.ShapeDtypeStruct((n, F * B), jnp.bfloat16),
            jax.ShapeDtypeStruct((2 * F, B, n), jnp.bfloat16),
        ),
        in_specs=[
            SMEM,
            whole(n, F * B),
            whole(1, F * B),
            pl.BlockSpec((8, B, B), lambda s: (s, 0, 0)),
            whole(B, B),
            whole(B, B),
        ],
        out_specs=(pl.BlockSpec((n, 8 * B), lambda s: (0, s)), whole(2 * F, B, n)),
        scratch_shapes=[
            pltpu.VMEM((n, B), jnp.float32),
            pltpu.VMEM((F, n, B), jnp.float32),
            pltpu.VMEM((F, n, B), jnp.bfloat16),
        ],
        compiler_params=pltpu.CompilerParams(vmem_limit_bytes=40 << 20),
        name="prologue",
    )(order, x, gain, w0, eye, take)


def stage_kernel(step, segments, first, *refs):
    (order_ref, cot_ref, inc_ref, x_ref, slope_ref, gain_ref, w1_ref, w0_ref) = refs[:8]
    refs = refs[8:] if first else refs[11:]
    (send_ref, right_ref, out_ref, part_ref) = refs[:4]
    (g_buf, x_buf, s_buf, w1_buf, w0_buf, low_buf, mid_buf, cg_buf, gp_buf, o_buf, p_buf, sem, sem1, sem0) = refs[4:]
    rows = g_buf.shape[0]
    position = lax.axis_index("segment")
    chunk = step - LAG * (segments - 1 - position)
    top = position == segments - 1
    valid = jnp.logical_and(chunk >= 0, chunk < CHUNKS)

    @pl.when(valid)
    def _():
        at_rows = pl.ds(pl.multiple_of(chunk * rows, rows), rows)

        @pl.when(top)
        def _():
            pltpu.make_async_copy(cot_ref.at[at_rows, :], g_buf, sem.at[0]).start()

        @pl.when(jnp.logical_not(top))
        def _():
            pltpu.make_async_copy(inc_ref, g_buf, sem.at[0]).start()

        w1_copies = [pltpu.make_async_copy(w1_ref.at[pl.ds(8 * k, 8)], w1_buf.at[pl.ds(8 * k, 8)], sem1.at[k]) for k in range(8)]
        w0_copies = [pltpu.make_async_copy(w0_ref.at[pl.ds(8 * k, 8)], w0_buf.at[pl.ds(8 * k, 8)], sem0.at[k]) for k in range(8)]
        x_copy = pltpu.make_async_copy(x_ref.at[at_rows, :], x_buf, sem.at[1])
        s_copy = pltpu.make_async_copy(slope_ref.at[at_rows, :], s_buf, sem.at[2])
        for k in range(8):
            w1_copies[k].start()
        x_copy.start()
        s_copy.start()
        for k in range(8):
            w0_copies[k].start()
        pltpu.make_async_copy(inc_ref, g_buf, sem.at[0]).wait()
        g_copy = pltpu.make_async_copy(g_buf, right_ref.at[at_rows, pl.ds(F * B, F * B)], sem.at[3])
        g_copy.start()

        @pl.loop(0, 8)
        def _(k):
            pltpu.make_async_copy(w1_ref.at[pl.ds(0, 8)], w1_buf.at[pl.ds(0, 8)], sem1.at[k]).wait()
            for i in range(8):
                j = 8 * k + i
                low_buf[order_ref[j]] = dot_nt(g_buf[:, col(j)], w1_buf[j])

        x_copy.wait()
        inv = inverse_rms(x_buf, slice(None))

        @pl.loop(0, 8)
        def _(k):
            parts = exchange([low_buf[8 * k + i] for i in range(8)], 1)
            for i in range(8):
                mid_buf[8 * i + k] = parts[i]

        s_copy.wait()
        for k in range(8):
            w0_copies[k].wait()

        def second(low, inner):
            parts = exchange([mid_buf[8 * low + g] for g in range(8)], 4)
            for g in range(8):
                j = 8 * g + low
                at = col(j)
                gp = (parts[g] * s_buf[:, at].astype(jnp.float32)).astype(jnp.bfloat16)
                gp_buf[:, at] = gp
                gh = dot_nt(gp, w0_buf[j])
                xh = x_buf[:, at].astype(jnp.float32) * inv
                term = gh * xh
                part = term[:8]
                for t in range(8, rows, 8):
                    part = part + term[t : t + 8]
                p_buf[:, at] = part
                gain = gain_ref[:, at]
                cg_buf[:, at] = gh * gain
                inner = inner + term * gain
            return inner

        inner = lax.fori_loop(0, 8, second, jnp.zeros((rows, B), jnp.float32))
        gp_copy = pltpu.make_async_copy(gp_buf, right_ref.at[at_rows, pl.ds(0, F * B)], sem.at[4])
        gp_copy.start()
        p_copy = pltpu.make_async_copy(p_buf, part_ref.at[chunk], sem.at[5])
        p_copy.start()
        inner = jnp.sum(inner, axis=1, keepdims=True) * (1.0 / (F * B))

        @pl.loop(0, F, unroll=8)
        def _(j):
            at = col(j)
            xh = x_buf[:, at].astype(jnp.float32) * inv
            o_buf[:, at] = (g_buf[:, at].astype(jnp.float32) + inv * (cg_buf[:, at] - xh * inner)).astype(jnp.bfloat16)

        o_copy = pltpu.make_async_copy(o_buf, send_ref, sem.at[6])
        o_copy.start()
        i_copy = pltpu.make_async_copy(o_buf, out_ref.at[at_rows, :], sem.at[7])
        i_copy.start()
        for copy in (g_copy, gp_copy, p_copy, o_copy, i_copy):
            copy.wait()


def stage(step, segments, order, cot, inc, x, slope, gain, w1, w0, carried):
    n = x.shape[0]
    rows = n // CHUNKS
    wide = F * B
    bf, f32 = jnp.bfloat16, jnp.float32
    first = carried is None
    args = [order, cot, inc, x, slope, gain, w1, w0] + ([] if first else list(carried))
    return pl.pallas_call(
        functools.partial(stage_kernel, step, segments, first),
        out_shape=(
            jax.ShapeDtypeStruct((rows, wide), bf),
            jax.ShapeDtypeStruct((n, 2 * wide), bf),
            jax.ShapeDtypeStruct((n, wide), bf),
            jax.ShapeDtypeStruct((CHUNKS, 8, wide), f32),
        ),
        in_specs=[SMEM] + [ANY] * 4 + [VMEM] + [ANY] * (2 if first else 5),
        out_specs=(ANY,) * 4,
        scratch_shapes=[
            pltpu.VMEM((rows, wide), bf),
            pltpu.VMEM((rows, wide), bf),
            pltpu.VMEM((rows, wide), bf),
            pltpu.VMEM((F, B, B), bf),
            pltpu.VMEM((F, B, B), bf),
            pltpu.VMEM((F, rows, B), f32),
            pltpu.VMEM((F, rows, B), f32),
            pltpu.VMEM((rows, wide), f32),
            pltpu.VMEM((rows, wide), bf),
            pltpu.VMEM((rows, wide), bf),
            pltpu.VMEM((8, wide), f32),
            pltpu.SemaphoreType.DMA((8,)),
            pltpu.SemaphoreType.DMA((8,)),
            pltpu.SemaphoreType.DMA((8,)),
        ],
        input_output_aliases={} if first else {8: 1, 9: 2, 10: 3},
        compiler_params=pltpu.CompilerParams(vmem_limit_bytes=24 << 20),
        cost_estimate=pl.CostEstimate(flops=4 * rows * wide * B, bytes_accessed=6 << 20, transcendentals=0),
        name="stage",
    )(*args)


def grads_kernel(scale, blocks, table_ref, perm_ref, left_ref, right_ref, part_ref, send_ref, keep_ref, s_buf, k_buf, sem):
    me = lax.axis_index("dp")
    half = F
    chunk_rows = 8 * B

    def rows_of(k, size=chunk_rows):
        return pl.ds(pl.multiple_of(k * chunk_rows, chunk_rows), size)

    for j in range(F):
        total = jnp.sum(jnp.sum(part_ref[:, :, j * B : (j + 1) * B], axis=0), axis=0, keepdims=True) * scale
        k_buf[half * B + j : half * B + j + 1, :] = total
    s_buf[half * B :, :] = k_buf[half * B :, :].astype(jnp.bfloat16)

    @pl.loop(0, 8)
    def _(k):
        for i in range(8):
            p = 8 * k + i
            which = table_ref[perm_ref[p] ^ (me * blocks)]
            value = dot(left_ref[which], right_ref[:, col(which)]) * scale
            s_buf[pl.ds(pl.multiple_of(p * B, B), B), :] = value.astype(jnp.bfloat16)
        pltpu.make_async_copy(s_buf.at[rows_of(k)], send_ref.at[rows_of(k)], sem.at[0]).start()

    @pl.loop(0, 8)
    def _(k):
        for i in range(8):
            p = 8 * k + i
            which = table_ref[perm_ref[half + p] ^ (me * blocks)]
            k_buf[pl.ds(pl.multiple_of(p * B, B), B), :] = dot(left_ref[which], right_ref[:, col(which)]) * scale
        pltpu.make_async_copy(k_buf.at[rows_of(k)], keep_ref.at[rows_of(k)], sem.at[1]).start()

    tail = pl.ds(half * B, F)
    pltpu.make_async_copy(s_buf.at[tail], send_ref.at[tail], sem.at[0]).start()
    pltpu.make_async_copy(k_buf.at[tail], keep_ref.at[tail], sem.at[1]).start()
    pltpu.make_async_copy(s_buf, send_ref, sem.at[0]).wait()
    pltpu.make_async_copy(k_buf, keep_ref, sem.at[1]).wait()


def grads(scale, blocks, table, perm, left, right, part):
    rows = F * B + F
    return pl.pallas_call(
        functools.partial(grads_kernel, scale, blocks),
        out_shape=(jax.ShapeDtypeStruct((rows, B), jnp.bfloat16), jax.ShapeDtypeStruct((rows, B), jnp.float32)),
        in_specs=[SMEM, SMEM, VMEM, VMEM, VMEM],
        out_specs=(ANY, ANY),
        scratch_shapes=[
            pltpu.VMEM((rows, B), jnp.bfloat16),
            pltpu.VMEM((rows, B), jnp.float32),
            pltpu.SemaphoreType.DMA((2,)),
        ],
        compiler_params=pltpu.CompilerParams(vmem_limit_bytes=40 << 20),
        name="grads",
    )(table, perm, left, right, part)


def order_of(bits, low_first):
    def place(q):
        digits = [(q >> k) & 1 for k in range(bits)]
        if not low_first:
            digits = digits[::-1]
        return [1 - d for d in digits]

    return sorted(range(1 << bits), key=place)


def swap(array, axis, bit):
    size = lax.axis_size(axis)
    return lax.ppermute(array, axis, [(i, i ^ (1 << bit)) for i in range(size)])


def reduce_owners(send, keep, dp, blocks):
    bits = dp.bit_length() - 2
    got = swap(send, "dp", 0)
    total = keep + got.astype(jnp.float32)
    first = max(blocks // 2, 1)
    cut = (dp // 2) * first * B
    sides = [(total[:cut], list(range(1, bits + 1))), (total[cut : F * B], list(range(bits, 0, -1)))]
    gain = total[F * B :]
    ends = []
    for index in range(bits):
        sent = []
        for side, bits_of in sides:
            half = side.shape[0] // 2
            if side.shape[0]:
                sent.append(swap(side[:half].astype(jnp.bfloat16), "dp", bits_of[index]))
            else:
                sent.append(None)
        got_gain = swap(gain, "dp", index + 1)
        gain = gain + got_gain
        sides = [
            (side[side.shape[0] // 2 :] + (0 if other is None else other.astype(jnp.float32)), bits_of)
            for (side, bits_of), other in zip(sides, sent)
        ]
    return jnp.concatenate([side for side, _ in sides], axis=0), gain


def local(acts, weights, gains, cotangent, block_order, owner_table):
    x = acts[0]
    n = x.shape[0]
    segments = lax.axis_size("segment")
    dp = lax.axis_size("dp")
    blocks = 2 * F // dp
    scale = 1.0 / math.sqrt(n * dp)
    w0 = weights[0, 0]
    w1 = weights[0, 1].reshape(F, 2, B // 2, B).swapaxes(1, 2).reshape(F, B, B)
    row = lax.broadcasted_iota(jnp.int32, (B, B), 0)
    column = lax.broadcasted_iota(jnp.int32, (B, B), 1)
    eye = (row == column).astype(jnp.bfloat16)
    take = (2 * (row % (B // 2)) + row // (B // 2) == column).astype(jnp.bfloat16)
    slope, left = prologue(block_order, x, gains, w0, eye, take)

    rows = n // CHUNKS
    steps = CHUNKS + LAG * (segments - 1)
    pairs = [(i, i - 1) for i in range(1, segments)]
    sent, carried = [], None
    for step in range(steps):
        inc = sent[step - LAG] if step >= LAG else cotangent[:rows]
        out = stage(step, segments, block_order, cotangent, inc, x, slope, gains, w1, w0, carried)
        carried = out[1:]
        if step < steps - LAG:
            sent.append(lax.ppermute(out[0], "segment", pairs))
    right, input_gradient, part = carried

    bits = dp.bit_length() - 2
    first = max(blocks // 2, 1)
    places = [(2 * q) * blocks + i for q in order_of(bits, True) for i in range(first)]
    places += [(2 * q) * blocks + i for q in order_of(bits, False) for i in range(first, blocks)]
    perm = jnp.array([p + blocks for p in places] + places, jnp.int32)
    send, keep = grads(scale, blocks, owner_table, perm, left, right, part)
    owned, gain = reduce_owners(send, keep, dp, blocks)
    width = F * B // dp
    own_gain = lax.dynamic_slice(gain.reshape(F * B), (lax.axis_index("dp") * width,), (width,))
    return input_gradient[None], owned.reshape(1, blocks, B, B), own_gain[None]


def solution(mesh):
    return jax.shard_map(
        local,
        mesh=mesh,
        in_specs=(
            P("segment", "dp", None),
            P("segment", None, None, None, None),
            P("segment", None),
            P("dp", None),
            P(),
            P(),
        ),
        out_specs=(P("segment", "dp", None), P("segment", "dp", None, None), P("segment", "dp")),
        check_vma=False,
    )
```

```python
import functools
import math

import jax
import jax.numpy as jnp
from jax import lax
from jax.experimental import pallas as pl
from jax.experimental.pallas import tpu as pltpu
from jax.sharding import PartitionSpec as P

F = 64
B = 128
EPS = 1e-05
CHUNKS = 8
LAG = 2
ANY = pl.BlockSpec(memory_space=pl.ANY)
VMEM = pl.BlockSpec(memory_space=pltpu.VMEM)
SMEM = pl.BlockSpec(memory_space=pltpu.SMEM)
TN = (((0,), (0,)), ((), ()))
LIMIT = 16 << 20


def dot(a, b):
    return jnp.dot(a, b, preferred_element_type=jnp.float32)


def dot_tn(a, b):
    return lax.dot_general(a, b, TN, preferred_element_type=jnp.float32)


def col(j):
    if isinstance(j, int):
        return pl.ds(j * B, B)
    return pl.ds(pl.multiple_of(j * B, B), B)


def exchange(parts, lane_bit):
    lane = lax.broadcasted_iota(jnp.int32, parts[0].shape, 1)
    parts = list(parts)
    for i in range(3):
        shift = 1 << (lane_bit + i)
        upper = (lane & shift) != 0
        for low in range(8):
            if low & (1 << i):
                continue
            high = low | (1 << i)
            a, b = parts[low], parts[high]
            parts[low] = jnp.where(upper, pltpu.roll(b, shift, 1), a)
            parts[high] = jnp.where(upper, b, pltpu.roll(a, B - shift, 1))
    return parts


def gelu_pair(v):
    cdf = 0.5 * (1.0 + lax.erf(v * 0.7071067811865476))
    density = jnp.exp(-0.5 * v * v) * 0.3989422804014327
    return v * cdf, cdf + v * density


def matrix(rule):
    row = lax.broadcasted_iota(jnp.int32, (B, B), 0)
    column = lax.broadcasted_iota(jnp.int32, (B, B), 1)
    return rule(row, column).astype(jnp.float32).astype(jnp.bfloat16)


def prepare_kernel(w_ref, w1_ref, w0_ref):
    half = B // 2
    mixed = matrix(lambda r, c: c == 2 * (r % half) + r // half)
    eye = matrix(lambda r, c: c == r)
    for j in range(F):
        w1_ref[j] = dot_tn(w_ref[1, j], mixed).astype(jnp.bfloat16)
    for j in range(F):
        w0_ref[j] = dot_tn(w_ref[0, j], eye).astype(jnp.bfloat16)


def prepare(weights):
    shape = jax.ShapeDtypeStruct((F, B, B), jnp.bfloat16)
    return pl.pallas_call(
        prepare_kernel,
        out_shape=(shape, shape),
        in_specs=[VMEM],
        out_specs=(VMEM, VMEM),
        compiler_params=pltpu.CompilerParams(vmem_limit_bytes=LIMIT),
        name="prepare",
    )(weights)


def span(plan, step, segments):
    position = lax.axis_index("segment")
    first = last = 0
    for p in range(segments):
        done, now = sum(plan[p][:step]), sum(plan[p][: step + 1])
        first = jnp.where(position == p, done, first)
        last = jnp.where(position == p, now, last)
    return first, last


def spread(pieces, slots, ready):
    plan = [0] * (max(slots) + 1)
    left = pieces
    for index, step in enumerate(slots):
        share = -(-left // (len(slots) - index))
        share = min(share, ready(step) - (pieces - left))
        plan[step] = share
        left -= share
    assert left == 0
    return plan


def plans(segments):
    steps = CHUNKS + LAG * (segments - 1)
    forward_plan, mix_plan = [], []
    for p in range(segments):
        begin = LAG * (segments - 1 - p)
        end = begin + CHUNKS
        if begin == 0:
            ahead = spread(CHUNKS, range(CHUNKS), lambda step: CHUNKS)
        else:
            ahead = spread(CHUNKS, range(min(begin, 4)), lambda step: CHUNKS)
        ahead += [0] * (steps - len(ahead))
        idle = [step for step in range(steps) if step < begin or step >= end]
        if begin == 0 or begin < steps - end:
            idle = [step for step in idle if step >= end][:4]
        blend = spread(CHUNKS // 2, idle[-4:], lambda step: sum(ahead[: step + 1]) // 2)
        blend += [0] * (steps - len(blend))
        forward_plan.append(ahead)
        mix_plan.append(blend)
    return forward_plan, mix_plan


def forward_kernel(step, plan, first, *refs):
    x_ref, gain_ref, w_ref = refs[:3]
    inv_ref, left_ref, z_ref, slope_ref, pre_buf = refs[3:] if first else refs[7:]
    rows = pre_buf.shape[0]

    @pl.loop(*span(plan, step, len(plan)))
    def _(chunk):
        at_rows = pl.ds(pl.multiple_of(chunk * rows, rows), rows)

        def square(j, total):
            v = x_ref[at_rows, col(j)].astype(jnp.float32)
            return total + v * v

        total = lax.fori_loop(0, F, square, jnp.zeros((rows, B), jnp.float32), unroll=16)
        mean = jnp.sum(total, axis=1, keepdims=True) * (1.0 / (F * B))
        inv = jnp.broadcast_to(lax.rsqrt(mean + EPS), (rows, B))
        inv_ref[at_rows, :] = inv

        @pl.loop(0, F, unroll=32)
        def _(j):
            h = (x_ref[at_rows, col(j)].astype(jnp.float32) * inv * gain_ref[:, col(j)]).astype(jnp.bfloat16)
            left_ref[at_rows, col(j)] = h
            pre_buf[:, col(j)] = dot(h, w_ref[0, j])

        @pl.loop(0, F, unroll=8)
        def _(j):
            z, slope = gelu_pair(pre_buf[:, col(j)])
            slope_ref[at_rows, col(j)] = slope
            z_ref[at_rows, col(j)] = z.astype(jnp.bfloat16)


def forward(step, plan, x, gain, weights, carried):
    n = x.shape[0]
    wide = F * B
    first = carried is None
    return pl.pallas_call(
        functools.partial(forward_kernel, step, plan, first),
        out_shape=(
            jax.ShapeDtypeStruct((n, B), jnp.float32),
            jax.ShapeDtypeStruct((n, 2 * wide), jnp.bfloat16),
            jax.ShapeDtypeStruct((n, wide), jnp.bfloat16),
            jax.ShapeDtypeStruct((n, wide), jnp.float32),
        ),
        in_specs=[VMEM] * (3 if first else 7),
        out_specs=(VMEM,) * 4,
        scratch_shapes=[pltpu.VMEM((n // CHUNKS, wide), jnp.float32)],
        input_output_aliases={} if first else {3: 0, 4: 1, 5: 2, 6: 3},
        compiler_params=pltpu.CompilerParams(vmem_limit_bytes=LIMIT),
        cost_estimate=pl.CostEstimate(flops=1 << 20, bytes_accessed=4 << 20, transcendentals=0),
        name="forward",
    )(x, gain, weights, *(() if first else carried))


def mix_kernel(step, plan, z_ref, old_ref, left_ref, low_buf, mid_buf):
    rows = low_buf.shape[1]
    half = B // 2
    apart = matrix(lambda r, c: c == r // 2 + half * (r % 2))

    @pl.loop(*span(plan, step, len(plan)))
    def _(pair):
        at_rows = pl.ds(pl.multiple_of(pair * rows, rows), rows)

        @pl.loop(0, F, unroll=8)
        def _(j):
            low_buf[j] = dot(z_ref[at_rows, col(j)], apart).astype(jnp.bfloat16)

        @pl.loop(0, 8, unroll=2)
        def _(k):
            parts = exchange([low_buf[8 * k + i] for i in range(8)], 0)
            for i in range(8):
                mid_buf[8 * i + k] = parts[i]

        @pl.loop(0, 8, unroll=2)
        def _(low):
            parts = exchange([mid_buf[8 * low + g] for g in range(8)], 3)
            for g in range(8):
                left_ref[at_rows, col(F + 8 * g + low)] = parts[g]


def mix(step, plan, z, left):
    n = z.shape[0]
    return pl.pallas_call(
        functools.partial(mix_kernel, step, plan),
        out_shape=jax.ShapeDtypeStruct((n, 2 * F * B), jnp.bfloat16),
        in_specs=[VMEM] * 2,
        out_specs=VMEM,
        scratch_shapes=[pltpu.VMEM((F, 2 * n // CHUNKS, B), jnp.bfloat16)] * 2,
        input_output_aliases={1: 0},
        compiler_params=pltpu.CompilerParams(vmem_limit_bytes=LIMIT),
        cost_estimate=pl.CostEstimate(flops=1 << 20, bytes_accessed=4 << 20, transcendentals=0),
        name="mix",
    )(z, left)


def stage_kernel(step, segments, first, *refs):
    (order_ref, cot_ref, inc_ref, x_ref, inv_ref, slope_ref, gain_ref, w1_ref, w0_ref) = refs[:9]
    refs = refs[9:] if first else refs[11:]
    (send_ref, right_ref, part_ref, g_buf, low_buf, mid_buf, gh_buf) = refs
    rows = g_buf.shape[0]
    wide = F * B
    position = lax.axis_index("segment")
    chunk = step - LAG * (segments - 1 - position)
    top = position == segments - 1

    @pl.when(jnp.logical_and(chunk >= 0, chunk < CHUNKS))
    def _():
        at_rows = pl.ds(pl.multiple_of(chunk * rows, rows), rows)

        @pl.when(top)
        def _():
            g_buf[...] = cot_ref[at_rows, :]

        @pl.when(jnp.logical_not(top))
        def _():
            g_buf[...] = inc_ref[...]

        for j in range(F):
            g = g_buf[:, col(j)]
            right_ref[at_rows, col(F + j)] = g
            low_buf[order_ref[j]] = dot(g, w1_ref[j]).astype(jnp.bfloat16)

        @pl.loop(0, 8, unroll=4)
        def _(k):
            parts = exchange([low_buf[8 * k + i] for i in range(8)], 1)
            for i in range(8):
                mid_buf[8 * i + k] = parts[i]

        @pl.loop(0, 8, unroll=4)
        def _(low):
            parts = exchange([mid_buf[8 * low + g] for g in range(8)], 4)
            for g in range(8):
                at = col(8 * g + low)
                right_ref[at_rows, at] = (parts[g].astype(jnp.float32) * slope_ref[at_rows, at]).astype(jnp.bfloat16)

        inv = inv_ref[at_rows, :]
        inner = jnp.zeros((rows, B), jnp.float32)
        for j in range(F):
            gh_buf[:, col(j)] = dot(right_ref[at_rows, col(j)], w0_ref[j])

        def weigh(j, inner):
            at = col(j)
            term = gh_buf[:, at] * (x_ref[at_rows, at].astype(jnp.float32) * inv)
            part = term[:8]
            for t in range(8, rows, 8):
                part = part + term[t : t + 8]
            part_ref[:, at] = jnp.where(chunk == 0, 0.0, part_ref[:, at]) + part
            return inner + term * gain_ref[:, at]

        inner = lax.fori_loop(0, F, weigh, inner, unroll=8)
        inner = jnp.sum(inner, axis=1, keepdims=True) * (1.0 / (F * B))

        @pl.loop(0, F, unroll=8)
        def _(j):
            at = col(j)
            xh = x_ref[at_rows, at].astype(jnp.float32) * inv
            value = g_buf[:, at].astype(jnp.float32) + inv * (gh_buf[:, at] * gain_ref[:, at] - xh * inner)
            value = value.astype(jnp.bfloat16)
            send_ref[:, at] = value
            right_ref[at_rows, col(2 * F + j)] = value


def stage(step, segments, order, cot, inc, x, inv, slope, gain, w1, w0, carried):
    n = x.shape[0]
    rows = n // CHUNKS
    wide = F * B
    bf, f32 = jnp.bfloat16, jnp.float32
    first = carried is None
    args = [order, cot, inc, x, inv, slope, gain, w1, w0] + ([] if first else list(carried))
    return pl.pallas_call(
        functools.partial(stage_kernel, step, segments, first),
        out_shape=(
            jax.ShapeDtypeStruct((rows, wide), bf),
            jax.ShapeDtypeStruct((n, 3 * wide), bf),
            jax.ShapeDtypeStruct((8, wide), f32),
        ),
        in_specs=[SMEM] + [VMEM] * (8 if first else 10),
        out_specs=(VMEM,) * 3,
        scratch_shapes=[
            pltpu.VMEM((rows, wide), bf),
            pltpu.VMEM((F, rows, B), bf),
            pltpu.VMEM((F, rows, B), bf),
            pltpu.VMEM((rows, wide), f32),
        ],
        input_output_aliases={} if first else {9: 1, 10: 2},
        compiler_params=pltpu.CompilerParams(vmem_limit_bytes=LIMIT),
        cost_estimate=pl.CostEstimate(flops=4 * rows * wide * B, bytes_accessed=6 << 20, transcendentals=0),
        name="stage",
    )(*args)


def grads_kernel(scale, blocks, table_ref, perm_ref, left_col_ref, left_ref, right_ref, part_ref, send_ref, keep_ref, grad_ref, s_buf, k_buf, sem):
    me = lax.axis_index("dp")
    half = F
    chunk_rows = 8 * B
    out = pltpu.make_async_copy(right_ref.at[:, pl.ds(2 * F * B, F * B)], grad_ref, sem.at[2])
    out.start()

    def rows_of(k, size=chunk_rows):
        return pl.ds(pl.multiple_of(k * chunk_rows, chunk_rows), size)

    for j in range(F):
        total = jnp.sum(part_ref[:, j * B : (j + 1) * B], axis=0, keepdims=True) * scale
        k_buf[half * B + j : half * B + j + 1, :] = total
    s_buf[half * B :, :] = k_buf[half * B :, :].astype(jnp.bfloat16)

    def product(p, buf, at):
        which = table_ref[perm_ref[p] ^ (me * blocks)]
        value = dot_tn(left_ref[:, col(left_col_ref[which])], right_ref[:, col(which)]) * scale
        buf[at, :] = value.astype(buf.dtype)

    for buf, ref, base, index in ((s_buf, send_ref, 0, 0), (k_buf, keep_ref, half, 1)):

        @pl.loop(0, 8)
        def _(k):
            for i in range(8):
                p = 8 * k + i
                product(base + p, buf, pl.ds(pl.multiple_of(p * B, B), B))
            pltpu.make_async_copy(buf.at[rows_of(k)], ref.at[rows_of(k)], sem.at[index]).start()

    tail = pl.ds(half * B, F)
    pltpu.make_async_copy(s_buf.at[tail], send_ref.at[tail], sem.at[0]).start()
    pltpu.make_async_copy(k_buf.at[tail], keep_ref.at[tail], sem.at[1]).start()
    pltpu.make_async_copy(s_buf, send_ref, sem.at[0]).wait()
    pltpu.make_async_copy(k_buf, keep_ref, sem.at[1]).wait()
    out.wait()


def grads(scale, blocks, table, perm, left_col, left, right, part):
    rows = F * B + F
    n = left.shape[0]
    return pl.pallas_call(
        functools.partial(grads_kernel, scale, blocks),
        out_shape=(
            jax.ShapeDtypeStruct((rows, B), jnp.bfloat16),
            jax.ShapeDtypeStruct((rows, B), jnp.float32),
            jax.ShapeDtypeStruct((n, F * B), jnp.bfloat16),
        ),
        in_specs=[SMEM, SMEM, SMEM, VMEM, VMEM, VMEM],
        out_specs=(ANY, ANY, ANY),
        scratch_shapes=[
            pltpu.VMEM((rows, B), jnp.bfloat16),
            pltpu.VMEM((rows, B), jnp.float32),
            pltpu.SemaphoreType.DMA((3,)),
        ],
        compiler_params=pltpu.CompilerParams(vmem_limit_bytes=LIMIT),
        name="grads",
    )(table, perm, left_col, left, right, part)


def order_of(bits, low_first):
    def place(q):
        digits = [(q >> k) & 1 for k in range(bits)]
        if not low_first:
            digits = digits[::-1]
        return [1 - d for d in digits]

    return sorted(range(1 << bits), key=place)


def swap(array, axis, bit):
    size = lax.axis_size(axis)
    return lax.ppermute(array, axis, [(i, i ^ (1 << bit)) for i in range(size)])


def reduce_owners(send, keep, dp, blocks):
    bits = dp.bit_length() - 2
    got = swap(send, "dp", 0)
    total = keep + got.astype(jnp.float32)
    first = max(blocks // 2, 1)
    cut = (dp // 2) * first * B
    sides = [(total[:cut], list(range(1, bits + 1))), (total[cut : F * B], list(range(bits, 0, -1)))]
    gain = total[F * B :]
    ends = []
    for index in range(bits):
        sent = []
        for side, bits_of in sides:
            half = side.shape[0] // 2
            if side.shape[0]:
                sent.append(swap(side[:half].astype(jnp.bfloat16), "dp", bits_of[index]))
            else:
                sent.append(None)
        got_gain = swap(gain, "dp", index + 1)
        gain = gain + got_gain
        sides = [
            (side[side.shape[0] // 2 :] + (0 if other is None else other.astype(jnp.float32)), bits_of)
            for (side, bits_of), other in zip(sides, sent)
        ]
    return jnp.concatenate([side for side, _ in sides], axis=0), gain


def local(acts, weights, gains, cotangent, block_order, owner_table):
    x = acts[0]
    n = x.shape[0]
    segments = lax.axis_size("segment")
    dp = lax.axis_size("dp")
    blocks = 2 * F // dp
    scale = 1.0 / math.sqrt(n * dp)
    rows = n // CHUNKS
    steps = CHUNKS + LAG * (segments - 1)
    pairs = [(i, i - 1) for i in range(1, segments)]
    w1, w0 = prepare(weights[0])
    forward_plan, mix_plan = plans(segments)
    sent, carried, ahead = [], None, None
    for step in range(steps):
        if any(plan[step] for plan in forward_plan):
            ahead = forward(step, forward_plan, x, gains, weights[0], ahead)
        inv, left, z, slope = ahead
        inc = sent[step - LAG] if step >= LAG else cotangent[:rows]
        out = stage(step, segments, block_order, cotangent, inc, x, inv, slope, gains, w1, w0, carried)
        carried = out[1:]
        if step < steps - LAG:
            sent.append(lax.ppermute(out[0], "segment", pairs))
        if any(plan[step] for plan in mix_plan):
            ahead = (inv, mix(step, mix_plan, z, left), z, slope)
    inv, left, z, slope = ahead
    right, part = carried

    bits = dp.bit_length() - 2
    first = max(blocks // 2, 1)
    places = [(2 * q) * blocks + i for q in order_of(bits, True) for i in range(first)]
    places += [(2 * q) * blocks + i for q in order_of(bits, False) for i in range(first, blocks)]
    perm = jnp.array([p + blocks for p in places] + places, jnp.int32)
    send, keep, input_gradient = grads(
        scale, blocks, owner_table, perm, jnp.concatenate([jnp.arange(F, dtype=jnp.int32), F + block_order]), left, right, part
    )
    owned, gain = reduce_owners(send, keep, dp, blocks)
    width = F * B // dp
    own_gain = lax.dynamic_slice(gain.reshape(F * B), (lax.axis_index("dp") * width,), (width,))
    return input_gradient[None], owned.reshape(1, blocks, B, B), own_gain[None]


def solution(mesh):
    return jax.shard_map(
        local,
        mesh=mesh,
        in_specs=(
            P("segment", "dp", None),
            P("segment", None, None, None, None),
            P("segment", None),
            P("dp", None),
            P(),
            P(),
        ),
        out_specs=(P("segment", "dp", None), P("segment", "dp", None, None), P("segment", "dp")),
        check_vma=False,
    )
```

```python
import functools
import math

import jax
import jax.numpy as jnp
from jax import lax
from jax.experimental import pallas as pl
from jax.experimental.pallas import tpu as pltpu
from jax.sharding import PartitionSpec as P

F = 64
B = 128
EPS = 1e-05
CHUNKS = 8
LAG = 2
AHEAD = 1
PREPARE_LIMIT = 46 << 20
ANY = pl.BlockSpec(memory_space=pl.ANY)
VMEM = pl.BlockSpec(memory_space=pltpu.VMEM)
HBM = pl.BlockSpec(memory_space=pltpu.HBM)
SMEM = pl.BlockSpec(memory_space=pltpu.SMEM)
TN = (((0,), (0,)), ((), ()))
LIMIT = 16 << 20


def dot(a, b):
    return jnp.dot(a, b, preferred_element_type=jnp.float32)


def dot_tn(a, b):
    return lax.dot_general(a, b, TN, preferred_element_type=jnp.float32)


def col(j):
    if isinstance(j, int):
        return pl.ds(j * B, B)
    return pl.ds(pl.multiple_of(j * B, B), B)


def exchange(parts, lane_bit):
    lane = lax.broadcasted_iota(jnp.int32, parts[0].shape, 1)
    parts = list(parts)
    for i in range(3):
        shift = 1 << (lane_bit + i)
        upper = (lane & shift) != 0
        for low in range(8):
            if low & (1 << i):
                continue
            high = low | (1 << i)
            a, b = parts[low], parts[high]
            parts[low] = jnp.where(upper, pltpu.roll(b, shift, 1), a)
            parts[high] = jnp.where(upper, b, pltpu.roll(a, B - shift, 1))
    return parts


def gelu_pair(v):
    cdf = 0.5 * (1.0 + lax.erf(v * 0.7071067811865476))
    density = jnp.exp(-0.5 * v * v) * 0.3989422804014327
    return v * cdf, cdf + v * density


def matrix(rule):
    row = lax.broadcasted_iota(jnp.int32, (B, B), 0)
    column = lax.broadcasted_iota(jnp.int32, (B, B), 1)
    return rule(row, column).astype(jnp.float32).astype(jnp.bfloat16)


def prepare_kernel(order_ref, w_ref, raw_ref, w1_ref, w0_ref, w_buf, sem):
    half = B // 2
    part = F // 4
    spans = [pl.ds(k * part, part) for k in range(4)]
    seconds = [pltpu.make_async_copy(w_ref.at[1, at], w_buf.at[at], sem.at[k]) for k, at in enumerate(spans)]
    firsts = [pltpu.make_async_copy(w_ref.at[0, at], raw_ref.at[at], sem.at[4 + k]) for k, at in enumerate(spans)]
    for copy in seconds + firsts:
        copy.start()
    mixed = matrix(lambda r, c: c == 2 * (r % half) + r // half)
    eye = matrix(lambda r, c: c == r)
    for k in range(4):
        seconds[k].wait()
        for j in range(k * part, (k + 1) * part):
            w1_ref[order_ref[j]] = dot_tn(w_buf[j], mixed).astype(jnp.bfloat16)
    for k in range(4):
        firsts[k].wait()
        for j in range(k * part, (k + 1) * part):
            w0_ref[j] = dot_tn(raw_ref[j], eye).astype(jnp.bfloat16)


def prepare(order, weights):
    bf = jnp.bfloat16
    factor = jax.ShapeDtypeStruct((F, B, B), bf)
    return pl.pallas_call(
        prepare_kernel,
        out_shape=(factor, factor, factor),
        in_specs=[SMEM, HBM],
        out_specs=(VMEM,) * 3,
        scratch_shapes=[pltpu.VMEM((F, B, B), bf), pltpu.SemaphoreType.DMA((8,))],
        compiler_params=pltpu.CompilerParams(vmem_limit_bytes=PREPARE_LIMIT),
        name="prepare",
    )(order, weights)


def shuffle_kernel(order_ref, cot_ref, out_ref):
    @pl.loop(0, F, unroll=4)
    def _(j):
        out_ref[:, col(order_ref[j])] = cot_ref[:, col(j)]


def shuffle(order, cotangent):
    return pl.pallas_call(
        shuffle_kernel,
        out_shape=jax.ShapeDtypeStruct(cotangent.shape, cotangent.dtype),
        in_specs=[SMEM, VMEM],
        out_specs=VMEM,
        compiler_params=pltpu.CompilerParams(vmem_limit_bytes=LIMIT),
        name="shuffle",
    )(order, cotangent)


def span(plan, step, ahead=0):
    position = lax.axis_index("segment")
    first = last = 0
    for p, pieces in enumerate(plan):
        first = jnp.where(position == p, sum(pieces[:step]), first)
        last = jnp.where(position == p, sum(pieces[: step + 1]), last)
    if ahead:
        total = sum(plan[-1])
        more = jnp.where(jnp.logical_and(position == len(plan) - 1, lax.axis_index("dp") % 2 == 1), ahead, 0)
        first = jnp.minimum(first + (more if step else 0), total)
        last = jnp.minimum(last + more, total)
    return first, last


def plans(segments):
    steps = CHUNKS + LAG * (segments - 1)
    forward_plan, mix_plan = [], []
    for p in range(segments):
        begin = LAG * (segments - 1 - p)
        ahead, blend = [0] * steps, [0] * steps
        if begin == 0:
            ahead[:CHUNKS] = [1] * CHUNKS
        elif begin < 4:
            ahead[:4] = [3, 3, 1, 1]
        else:
            ahead[:3] = [3, 3, 2]
        if begin >= 6:
            blend[3:5] = [2, 2]
        else:
            blend[steps - LAG - 1] = CHUNKS // 2
        forward_plan.append(ahead)
        mix_plan.append(blend)
    return forward_plan, mix_plan


def forward_kernel(step, plan, first, *refs):
    x_ref, gain_ref, w_ref = refs[:3]
    inv_ref, left_ref, z_ref, slope_ref, xh_ref, pre_buf = refs[3:] if first else refs[8:]
    rows = pre_buf.shape[0]

    @pl.loop(*span(plan, step, AHEAD))
    def _(chunk):
        at_rows = pl.ds(pl.multiple_of(chunk * rows, rows), rows)

        def square(j, total):
            v = x_ref[at_rows, col(j)].astype(jnp.float32)
            return total + v * v

        total = lax.fori_loop(0, F, square, jnp.zeros((rows, B), jnp.float32), unroll=16)
        mean = jnp.sum(total, axis=1, keepdims=True) * (1.0 / (F * B))
        inv = jnp.broadcast_to(lax.rsqrt(mean + EPS), (rows, B))
        inv_ref[at_rows, :] = inv

        @pl.loop(0, F, unroll=32)
        def _(j):
            xh = x_ref[at_rows, col(j)].astype(jnp.float32) * inv
            xh_ref[at_rows, col(j)] = xh
            h = (xh * gain_ref[:, col(j)]).astype(jnp.bfloat16)
            left_ref[at_rows, col(j)] = h
            pre_buf[:, col(j)] = dot(h, w_ref[j])

        @pl.loop(0, F, unroll=8)
        def _(j):
            z, slope = gelu_pair(pre_buf[:, col(j)])
            slope_ref[at_rows, col(j)] = slope
            z_ref[at_rows, col(j)] = z.astype(jnp.bfloat16)


def forward(step, plan, x, gain, w0, carried):
    n = x.shape[0]
    wide = F * B
    first = carried is None
    return pl.pallas_call(
        functools.partial(forward_kernel, step, plan, first),
        out_shape=(
            jax.ShapeDtypeStruct((n, B), jnp.float32),
            jax.ShapeDtypeStruct((n, 2 * wide), jnp.bfloat16),
            jax.ShapeDtypeStruct((n, wide), jnp.bfloat16),
            jax.ShapeDtypeStruct((n, wide), jnp.float32),
            jax.ShapeDtypeStruct((n, wide), jnp.float32),
        ),
        in_specs=[VMEM] * (3 if first else 8),
        out_specs=(VMEM,) * 5,
        scratch_shapes=[pltpu.VMEM((n // CHUNKS, wide), jnp.float32)],
        input_output_aliases={} if first else {3: 0, 4: 1, 5: 2, 6: 3, 7: 4},
        compiler_params=pltpu.CompilerParams(vmem_limit_bytes=LIMIT),
        cost_estimate=pl.CostEstimate(flops=1 << 20, bytes_accessed=4 << 20, transcendentals=0),
        name="forward",
    )(x, gain, w0, *(() if first else carried))


def mix_kernel(step, plan, z_ref, old_ref, left_ref, low_buf, mid_buf):
    rows = low_buf.shape[1]
    half = B // 2
    apart = matrix(lambda r, c: c == r // 2 + half * (r % 2))

    @pl.loop(*span(plan, step))
    def _(pair):
        at_rows = pl.ds(pl.multiple_of(pair * rows, rows), rows)

        @pl.loop(0, F, unroll=32)
        def _(j):
            low_buf[j] = dot(z_ref[at_rows, col(j)], apart).astype(jnp.bfloat16)

        @pl.loop(0, 8, unroll=4)
        def _(k):
            parts = exchange([low_buf[8 * k + i] for i in range(8)], 0)
            for i in range(8):
                mid_buf[8 * i + k] = parts[i]

        @pl.loop(0, 8, unroll=4)
        def _(low):
            parts = exchange([mid_buf[8 * low + g] for g in range(8)], 3)
            for g in range(8):
                left_ref[at_rows, col(F + 8 * g + low)] = parts[g]


def mix(step, plan, z, left):
    n = z.shape[0]
    return pl.pallas_call(
        functools.partial(mix_kernel, step, plan),
        out_shape=jax.ShapeDtypeStruct((n, 2 * F * B), jnp.bfloat16),
        in_specs=[VMEM] * 2,
        out_specs=VMEM,
        scratch_shapes=[pltpu.VMEM((F, 2 * n // CHUNKS, B), jnp.bfloat16)] * 2,
        input_output_aliases={1: 0},
        compiler_params=pltpu.CompilerParams(vmem_limit_bytes=LIMIT),
        cost_estimate=pl.CostEstimate(flops=1 << 20, bytes_accessed=4 << 20, transcendentals=0),
        name="mix",
    )(z, left)


def stage_kernel(step, segments, first, *refs):
    (order_ref, cot_ref, inc_ref, xh_ref, inv_ref, slope_ref, gain_ref, w1_ref, w0_ref) = refs[:9]
    refs = refs[10:] if first else refs[12:]
    (send_ref, right_ref, part_ref, g_buf, mid_buf, gh_buf, order_buf, sem) = refs
    rows = g_buf.shape[0]
    wide = F * B
    position = lax.axis_index("segment")
    chunk = step - LAG * (segments - 1 - position)
    top = position == segments - 1
    if first:
        part_ref[...] = jnp.zeros_like(part_ref)

    @pl.when(jnp.logical_and(chunk >= 0, chunk < CHUNKS))
    def _():
        at_rows = pl.ds(pl.multiple_of(chunk * rows, rows), rows)
        order_copy = pltpu.make_async_copy(order_ref, order_buf, sem)
        order_copy.start()

        @pl.when(top)
        def _():
            g_buf[...] = cot_ref[at_rows, :]

        @pl.when(jnp.logical_not(top))
        def _():
            g_buf[...] = inc_ref[...]

        for k in range(8):
            parts = [dot(g_buf[:, col(8 * k + i)], w1_ref[8 * k + i]).astype(jnp.bfloat16) for i in range(8)]
            parts = exchange(parts, 1)
            for i in range(8):
                mid_buf[8 * i + k] = parts[i]
                right_ref[at_rows, col(F + 8 * k + i)] = g_buf[:, col(8 * k + i)]

        inner = jnp.zeros((rows, B), jnp.float32)
        for low in range(8):
            parts = exchange([mid_buf[8 * low + g] for g in range(8)], 4)
            for g in range(8):
                at = col(8 * g + low)
                gp = (parts[g].astype(jnp.float32) * slope_ref[at_rows, at]).astype(jnp.bfloat16)
                right_ref[at_rows, at] = gp
                gh = dot(gp, w0_ref[8 * g + low])
                gh_buf[:, at] = gh
                term = gh * xh_ref[at_rows, at]
                part = term[:8]
                for t in range(8, rows, 8):
                    part = part + term[t : t + 8]
                part_ref[:, at] = part_ref[:, at] + part
                inner = inner + term * gain_ref[:, at]

        inner = jnp.sum(inner, axis=1, keepdims=True) * (1.0 / (F * B))
        inv = inv_ref[at_rows, :]
        inner = inner * inv
        order_copy.wait()

        @pl.loop(0, F, unroll=8)
        def _(j):
            at = col(j)
            to = col(order_buf[j])
            value = g_buf[:, to].astype(jnp.float32) + (inv * gain_ref[:, at]) * gh_buf[:, at] - xh_ref[at_rows, at] * inner
            value = value.astype(jnp.bfloat16)
            send_ref[:, to] = value
            right_ref[at_rows, col(2 * F + j)] = value


def stage(step, segments, order, cot, inc, xh, inv, slope, gain, w1, w0, left, carried):
    n = xh.shape[0]
    rows = n // CHUNKS
    wide = F * B
    bf, f32 = jnp.bfloat16, jnp.float32
    first = carried is None
    args = [order, cot, inc, xh, inv, slope, gain, w1, w0, left] + ([] if first else list(carried))
    return pl.pallas_call(
        functools.partial(stage_kernel, step, segments, first),
        out_shape=(
            jax.ShapeDtypeStruct((rows, wide), bf),
            jax.ShapeDtypeStruct((n, 3 * wide), bf),
            jax.ShapeDtypeStruct((8, wide), f32),
        ),
        in_specs=[ANY] + [VMEM] * (9 if first else 11),
        out_specs=(VMEM,) * 3,
        scratch_shapes=[
            pltpu.VMEM((rows, wide), bf),
            pltpu.VMEM((F, rows, B), bf),
            pltpu.VMEM((rows, wide), f32),
            pltpu.SMEM((F,), jnp.int32),
            pltpu.SemaphoreType.DMA,
        ],
        input_output_aliases={} if first else {10: 1, 11: 2},
        compiler_params=pltpu.CompilerParams(vmem_limit_bytes=LIMIT),
        cost_estimate=pl.CostEstimate(flops=4 * rows * wide * B, bytes_accessed=6 << 20, transcendentals=0),
        name="stage",
    )(*args)


def product(scale, blocks, p, table_ref, perm_ref, column_ref, left_ref, right_ref):
    which = table_ref[perm_ref[p] ^ (lax.axis_index("dp") * blocks)]
    at = col(column_ref[which])
    return dot_tn(left_ref[:, at], right_ref[:, at]) * scale


def gain_row(part_ref, scale, j):
    return jnp.sum(part_ref[:, j * B : (j + 1) * B], axis=0, keepdims=True) * scale


def sent_kernel(scale, blocks, table_ref, perm_ref, column_ref, left_ref, right_ref, part_ref, send_ref, gain_ref):
    for j in range(F):
        gain_ref[j : j + 1, :] = gain_row(part_ref, scale, j)
    send_ref[F * B :, :] = gain_ref[...].astype(jnp.bfloat16)

    @pl.loop(0, F, unroll=8)
    def _(p):
        value = product(scale, blocks, p, table_ref, perm_ref, column_ref, left_ref, right_ref)
        send_ref[pl.ds(pl.multiple_of(p * B, B), B), :] = value.astype(jnp.bfloat16)


def kept_kernel(scale, blocks, table_ref, perm_ref, column_ref, left_ref, right_ref, keep_ref, grad_ref, sem):
    out = pltpu.make_async_copy(right_ref.at[:, pl.ds(2 * F * B, F * B)], grad_ref, sem)
    out.start()

    @pl.loop(0, F, unroll=8)
    def _(p):
        value = product(scale, blocks, F + p, table_ref, perm_ref, column_ref, left_ref, right_ref)
        keep_ref[pl.ds(pl.multiple_of(p * B, B), B), :] = value

    out.wait()


def grads(scale, blocks, table, perm, column, left, right, part):
    n = left.shape[0]
    params = pltpu.CompilerParams(vmem_limit_bytes=LIMIT)
    f32 = jnp.float32
    cost = pl.CostEstimate(flops=2 * n * B * B * F, bytes_accessed=8 << 20, transcendentals=0)
    send, gain = pl.pallas_call(
        functools.partial(sent_kernel, scale, blocks),
        out_shape=(jax.ShapeDtypeStruct((F * B + F, B), jnp.bfloat16), jax.ShapeDtypeStruct((F, B), f32)),
        in_specs=[SMEM] * 3 + [VMEM] * 3,
        out_specs=(VMEM, VMEM),
        compiler_params=params,
        cost_estimate=cost,
        name="sent",
    )(table, perm, column, left, right, part)
    got = swap(send, 0)
    keep, input_gradient = pl.pallas_call(
        functools.partial(kept_kernel, scale, blocks),
        out_shape=(jax.ShapeDtypeStruct((F * B, B), f32), jax.ShapeDtypeStruct((n, F * B), jnp.bfloat16)),
        in_specs=[SMEM] * 3 + [VMEM] * 2,
        out_specs=(VMEM, ANY),
        scratch_shapes=[pltpu.SemaphoreType.DMA],
        compiler_params=params,
        cost_estimate=cost,
        name="kept",
    )(table, perm, column, left, right)
    return got, gain, keep, input_gradient


def split_kernel(sizes, offsets, *refs):
    count = len(sizes)
    keeps, gots, gain_ref = refs[:count], refs[count : 2 * count], refs[2 * count]
    sends, rest, total_ref = refs[2 * count + 1 : 3 * count + 1], refs[3 * count + 1 : 4 * count + 1], refs[4 * count + 1]
    f32 = jnp.float32
    for side in range(count):
        half = sizes[side] // 2
        for begin, target in ((0, sends[side]), (half, rest[side])):

            def body(k, side=side, begin=begin, target=target):
                piece = math.gcd(half, 256)
                at = pl.ds(pl.multiple_of(begin + k * piece + offsets[side], piece), piece)
                to = pl.ds(pl.multiple_of(k * piece, piece), piece)
                target[to, :] = (keeps[side][at, :] + gots[side][at, :].astype(f32)).astype(target.dtype)

            pl.loop(0, half // math.gcd(half, 256))(body)
    tail = gots[0].shape[0] - F
    total = gain_ref[...] + gots[0][tail:, :].astype(f32)
    total_ref[...] = total
    sends[0][sizes[0] // 2 :, :] = total.astype(jnp.bfloat16)


def split(sizes, offsets, keeps, gots, gain):
    f32 = jnp.float32
    halves = [size // 2 for size in sizes]
    outs = [jax.ShapeDtypeStruct((half + (F if side == 0 else 0), B), jnp.bfloat16) for side, half in enumerate(halves)]
    outs += [jax.ShapeDtypeStruct((half, B), f32) for half in halves] + [jax.ShapeDtypeStruct((F, B), f32)]
    got = pl.pallas_call(
        functools.partial(split_kernel, sizes, offsets),
        out_shape=tuple(outs),
        in_specs=[VMEM] * (2 * len(sizes) + 1),
        out_specs=(VMEM,) * len(outs),
        compiler_params=pltpu.CompilerParams(vmem_limit_bytes=LIMIT),
        name="split",
    )(*keeps, *gots, gain)
    count = len(sizes)
    return got[:count], got[count : 2 * count], got[-1]


def last_kernel(sizes, offsets, dp, *refs):
    count = len(sizes)
    keeps, gots, gain_ref = refs[:count], refs[count : 2 * count], refs[2 * count]
    out_ref, own_ref, gain_buf = refs[2 * count + 1 :]
    f32 = jnp.float32
    start = 0
    for side in range(count):
        piece = math.gcd(sizes[side], 256)

        @pl.loop(0, sizes[side] // piece)
        def _(k):
            at = pl.ds(pl.multiple_of(k * piece + offsets[side], piece), piece)
            to = pl.ds(pl.multiple_of(k * piece + start, piece), piece)
            out_ref[to, :] = keeps[side][at, :] + gots[side][at, :].astype(f32)

        start += sizes[side]
    tail = gots[0].shape[0] - F
    gain_buf[...] = gain_ref[...] + gots[0][tail:, :].astype(f32)
    each = F // dp
    me = lax.axis_index("dp")
    for r in range(each):
        own_ref[:, r * B : (r + 1) * B] = gain_buf[pl.ds(me * each + r, 1), :]


def last(sizes, offsets, dp, keeps, gots, gain):
    f32 = jnp.float32
    return pl.pallas_call(
        functools.partial(last_kernel, sizes, offsets, dp),
        out_shape=(jax.ShapeDtypeStruct((sum(sizes), B), f32), jax.ShapeDtypeStruct((1, F * B // dp), f32)),
        in_specs=[VMEM] * (2 * len(sizes) + 1),
        out_specs=(VMEM, VMEM),
        scratch_shapes=[pltpu.VMEM((F, B), f32)],
        compiler_params=pltpu.CompilerParams(vmem_limit_bytes=LIMIT),
        name="last",
    )(*keeps, *gots, gain)


def order_of(bits, low_first):
    def place(q):
        digits = [(q >> k) & 1 for k in range(bits)]
        if not low_first:
            digits = digits[::-1]
        return [1 - d for d in digits]

    return sorted(range(1 << bits), key=place)


def swap(array, bit):
    size = lax.axis_size("dp")
    return lax.ppermute(array, "dp", [(i, i ^ (1 << bit)) for i in range(size)])


def reduce_owners(got, gain, keep, dp, blocks):
    bits = dp.bit_length() - 2
    cut = (dp // 2) * max(blocks // 2, 1) * B
    sizes, offsets = [cut, F * B - cut], [0, cut]
    keeps, gots = [keep, keep], [got, got]
    for index in range(bits):
        sends, keeps, gain = split(sizes, offsets, keeps, gots, gain)
        gots = [swap(sends[0], index + 1), swap(sends[1], bits - index)]
        sizes, offsets = [size // 2 for size in sizes], [0, 0]
    return last(sizes, offsets, dp, keeps, gots, gain)


def local(acts, weights, gains, cotangent, block_order, owner_table):
    x = acts[0]
    n = x.shape[0]
    segments = lax.axis_size("segment")
    dp = lax.axis_size("dp")
    blocks = 2 * F // dp
    scale = 1.0 / math.sqrt(n * dp)
    rows = n // CHUNKS
    steps = CHUNKS + LAG * (segments - 1)
    pairs = [(i, i - 1) for i in range(1, segments)]
    raw, w1, w0 = prepare(block_order, weights[0])
    cot = shuffle(block_order, cotangent)
    forward_plan, mix_plan = plans(segments)
    sent, carried, ahead = [], None, None
    for step in range(steps):
        if any(plan[step] for plan in forward_plan):
            ahead = forward(step, forward_plan, x, gains, raw, ahead)
        inv, left, z, slope, xh = ahead
        inc = sent[step - LAG] if step >= LAG else cot[:rows]
        out = stage(step, segments, block_order, cot, inc, xh, inv, slope, gains, w1, w0, left, carried)
        carried = out[1:]
        if step < steps - LAG:
            sent.append(lax.ppermute(out[0], "segment", pairs))
        if any(plan[step] for plan in mix_plan):
            ahead = (inv, mix(step, mix_plan, z, left), z, slope, xh)
    left = ahead[1]
    right, part = carried

    bits = dp.bit_length() - 2
    first = max(blocks // 2, 1)
    places = [(2 * q) * blocks + i for q in order_of(bits, True) for i in range(first)]
    places += [(2 * q) * blocks + i for q in order_of(bits, False) for i in range(first, blocks)]
    perm = jnp.array([p + blocks for p in places] + places, jnp.int32)
    column = jnp.concatenate([jnp.arange(F, dtype=jnp.int32), F + block_order])
    got, gain, keep, input_gradient = grads(scale, blocks, owner_table, perm, column, left, right, part)
    owned, own_gain = reduce_owners(got, gain, keep, dp, blocks)
    return input_gradient[None], owned.reshape(1, blocks, B, B), own_gain


def solution(mesh):
    return jax.shard_map(
        local,
        mesh=mesh,
        in_specs=(
            P("segment", "dp", None),
            P("segment", None, None, None, None),
            P("segment", None),
            P("dp", None),
            P(),
            P(),
        ),
        out_specs=(P("segment", "dp", None), P("segment", "dp", None, None), P("segment", "dp")),
        check_vma=False,
    )
```

```python
import functools
import math

import jax
import jax.numpy as jnp
from jax import lax
from jax.experimental import pallas as pl
from jax.experimental.pallas import tpu as pltpu
from jax.sharding import PartitionSpec as P

F = 64
B = 128
EPS = 1e-05
CHUNKS = 8
LAG = 2
AHEAD = 1
PREPARE_LIMIT = 46 << 20
ANY = pl.BlockSpec(memory_space=pl.ANY)
VMEM = pl.BlockSpec(memory_space=pltpu.VMEM)
HBM = pl.BlockSpec(memory_space=pltpu.HBM)
SMEM = pl.BlockSpec(memory_space=pltpu.SMEM)
TN = (((0,), (0,)), ((), ()))
LIMIT = 16 << 20


def dot(a, b):
    return jnp.dot(a, b, preferred_element_type=jnp.float32)


def dot_tn(a, b):
    return lax.dot_general(a, b, TN, preferred_element_type=jnp.float32)


def col(j):
    if isinstance(j, int):
        return pl.ds(j * B, B)
    return pl.ds(pl.multiple_of(j * B, B), B)


def exchange(parts, lane_bit):
    lane = lax.broadcasted_iota(jnp.int32, parts[0].shape, 1)
    parts = list(parts)
    for i in range(3):
        shift = 1 << (lane_bit + i)
        upper = (lane & shift) != 0
        for low in range(8):
            if low & (1 << i):
                continue
            high = low | (1 << i)
            a, b = parts[low], parts[high]
            parts[low] = jnp.where(upper, pltpu.roll(b, shift, 1), a)
            parts[high] = jnp.where(upper, b, pltpu.roll(a, B - shift, 1))
    return parts


def gelu_pair(v):
    cdf = 0.5 * (1.0 + lax.erf(v * 0.7071067811865476))
    density = jnp.exp(-0.5 * v * v) * 0.3989422804014327
    return v * cdf, cdf + v * density


def matrix(rule):
    row = lax.broadcasted_iota(jnp.int32, (B, B), 0)
    column = lax.broadcasted_iota(jnp.int32, (B, B), 1)
    return rule(row, column).astype(jnp.float32).astype(jnp.bfloat16)


def prepare_kernel(order_ref, w_ref, raw_ref, w1_ref, w0_ref, w_buf, sem):
    half = B // 2
    part = F // 4
    spans = [pl.ds(k * part, part) for k in range(4)]
    seconds = [pltpu.make_async_copy(w_ref.at[1, at], w_buf.at[at], sem.at[k]) for k, at in enumerate(spans)]
    firsts = [pltpu.make_async_copy(w_ref.at[0, at], raw_ref.at[at], sem.at[4 + k]) for k, at in enumerate(spans)]
    for copy in seconds + firsts:
        copy.start()
    mixed = matrix(lambda r, c: c == 2 * (r % half) + r // half)
    eye = matrix(lambda r, c: c == r)
    for k in range(4):
        seconds[k].wait()
        for j in range(k * part, (k + 1) * part):
            w1_ref[order_ref[j]] = dot_tn(w_buf[j], mixed).astype(jnp.bfloat16)
    for k in range(4):
        firsts[k].wait()
        for j in range(k * part, (k + 1) * part):
            w0_ref[j] = dot_tn(raw_ref[j], eye).astype(jnp.bfloat16)


def prepare(order, weights):
    bf = jnp.bfloat16
    factor = jax.ShapeDtypeStruct((F, B, B), bf)
    return pl.pallas_call(
        prepare_kernel,
        out_shape=(factor, factor, factor),
        in_specs=[SMEM, HBM],
        out_specs=(VMEM,) * 3,
        scratch_shapes=[pltpu.VMEM((F, B, B), bf), pltpu.SemaphoreType.DMA((8,))],
        compiler_params=pltpu.CompilerParams(vmem_limit_bytes=PREPARE_LIMIT),
        name="prepare",
    )(order, weights)


def shuffle_kernel(order_ref, cot_ref, out_ref):
    @pl.loop(0, F, unroll=4)
    def _(j):
        out_ref[:, col(order_ref[j])] = cot_ref[:, col(j)]


def shuffle(order, cotangent):
    return pl.pallas_call(
        shuffle_kernel,
        out_shape=jax.ShapeDtypeStruct(cotangent.shape, cotangent.dtype),
        in_specs=[SMEM, VMEM],
        out_specs=VMEM,
        compiler_params=pltpu.CompilerParams(vmem_limit_bytes=LIMIT),
        name="shuffle",
    )(order, cotangent)


def span(plan, step, ahead=0):
    position = lax.axis_index("segment")
    first = last = 0
    for p, pieces in enumerate(plan):
        first = jnp.where(position == p, sum(pieces[:step]), first)
        last = jnp.where(position == p, sum(pieces[: step + 1]), last)
    if ahead:
        total = sum(plan[-1])
        more = jnp.where(jnp.logical_and(position == len(plan) - 1, lax.axis_index("dp") % 2 == 1), ahead, 0)
        first = jnp.minimum(first + (more if step else 0), total)
        last = jnp.minimum(last + more, total)
    return first, last


def plans(segments):
    steps = CHUNKS + LAG * (segments - 1)
    forward_plan, mix_plan = [], []
    for p in range(segments):
        begin = LAG * (segments - 1 - p)
        ahead, blend = [0] * steps, [0] * steps
        if begin == 0:
            ahead[:CHUNKS] = [1] * CHUNKS
        elif begin < 4:
            ahead[:4] = [3, 3, 1, 1]
        else:
            ahead[:3] = [3, 3, 2]
        if begin >= 6:
            blend[3:5] = [2, 2]
        else:
            blend[steps - LAG - 1] = CHUNKS // 2
        forward_plan.append(ahead)
        mix_plan.append(blend)
    return forward_plan, mix_plan


def forward_kernel(step, plan, first, *refs):
    x_ref, gain_ref, w_ref = refs[:3]
    inv_ref, left_ref, z_ref, slope_ref, xh_ref, pre_buf = refs[3:] if first else refs[8:]
    rows = pre_buf.shape[0]

    @pl.loop(*span(plan, step, AHEAD))
    def _(chunk):
        at_rows = pl.ds(pl.multiple_of(chunk * rows, rows), rows)

        def square(j, total):
            v = x_ref[at_rows, col(j)].astype(jnp.float32)
            return total + v * v

        total = lax.fori_loop(0, F, square, jnp.zeros((rows, B), jnp.float32), unroll=8)
        mean = jnp.sum(total, axis=1, keepdims=True) * (1.0 / (F * B))
        inv = jnp.broadcast_to(lax.rsqrt(mean + EPS), (rows, B))
        inv_ref[at_rows, :] = inv

        @pl.loop(0, F, unroll=32)
        def _(j):
            xh = x_ref[at_rows, col(j)].astype(jnp.float32) * inv
            xh_ref[at_rows, col(j)] = xh
            h = (xh * gain_ref[:, col(j)]).astype(jnp.bfloat16)
            left_ref[at_rows, col(j)] = h
            pre_buf[:, col(j)] = dot(h, w_ref[j])

        @pl.loop(0, F, unroll=8)
        def _(j):
            z, slope = gelu_pair(pre_buf[:, col(j)])
            slope_ref[at_rows, col(j)] = slope
            z_ref[at_rows, col(j)] = z.astype(jnp.bfloat16)


def forward(step, plan, x, gain, w0, carried):
    n = x.shape[0]
    wide = F * B
    first = carried is None
    return pl.pallas_call(
        functools.partial(forward_kernel, step, plan, first),
        out_shape=(
            jax.ShapeDtypeStruct((n, B), jnp.float32),
            jax.ShapeDtypeStruct((n, 2 * wide), jnp.bfloat16),
            jax.ShapeDtypeStruct((n, wide), jnp.bfloat16),
            jax.ShapeDtypeStruct((n, wide), jnp.float32),
            jax.ShapeDtypeStruct((n, wide), jnp.float32),
        ),
        in_specs=[VMEM] * (3 if first else 8),
        out_specs=(VMEM,) * 5,
        scratch_shapes=[pltpu.VMEM((n // CHUNKS, wide), jnp.float32)],
        input_output_aliases={} if first else {3: 0, 4: 1, 5: 2, 6: 3, 7: 4},
        compiler_params=pltpu.CompilerParams(vmem_limit_bytes=LIMIT),
        cost_estimate=pl.CostEstimate(flops=1 << 20, bytes_accessed=4 << 20, transcendentals=0),
        name="forward",
    )(x, gain, w0, *(() if first else carried))


def mix_kernel(step, plan, z_ref, old_ref, left_ref, low_buf, mid_buf):
    rows = low_buf.shape[1]
    half = B // 2
    apart = matrix(lambda r, c: c == r // 2 + half * (r % 2))

    @pl.loop(*span(plan, step))
    def _(pair):
        at_rows = pl.ds(pl.multiple_of(pair * rows, rows), rows)

        @pl.loop(0, F, unroll=32)
        def _(j):
            low_buf[j] = dot(z_ref[at_rows, col(j)], apart).astype(jnp.bfloat16)

        @pl.loop(0, 8, unroll=4)
        def _(k):
            parts = exchange([low_buf[8 * k + i] for i in range(8)], 0)
            for i in range(8):
                mid_buf[8 * i + k] = parts[i]

        @pl.loop(0, 8, unroll=4)
        def _(low):
            parts = exchange([mid_buf[8 * low + g] for g in range(8)], 3)
            for g in range(8):
                left_ref[at_rows, col(F + 8 * g + low)] = parts[g]


def mix(step, plan, z, left):
    n = z.shape[0]
    return pl.pallas_call(
        functools.partial(mix_kernel, step, plan),
        out_shape=jax.ShapeDtypeStruct((n, 2 * F * B), jnp.bfloat16),
        in_specs=[VMEM] * 2,
        out_specs=VMEM,
        scratch_shapes=[pltpu.VMEM((F, 2 * n // CHUNKS, B), jnp.bfloat16)] * 2,
        input_output_aliases={1: 0},
        compiler_params=pltpu.CompilerParams(vmem_limit_bytes=LIMIT),
        cost_estimate=pl.CostEstimate(flops=1 << 20, bytes_accessed=4 << 20, transcendentals=0),
        name="mix",
    )(z, left)


def stage_kernel(step, segments, first, *refs):
    (order_ref, cot_ref, inc_ref, xh_ref, inv_ref, slope_ref, gain_ref, w1_ref, w0_ref) = refs[:9]
    refs = refs[10:] if first else refs[12:]
    (send_ref, right_ref, part_ref, g_buf, mid_buf, gh_buf, order_buf, sem) = refs
    rows = g_buf.shape[0]
    wide = F * B
    position = lax.axis_index("segment")
    chunk = step - LAG * (segments - 1 - position)
    top = position == segments - 1
    if first:
        part_ref[...] = jnp.zeros_like(part_ref)

    @pl.when(jnp.logical_and(chunk >= 0, chunk < CHUNKS))
    def _():
        at_rows = pl.ds(pl.multiple_of(chunk * rows, rows), rows)
        order_copy = pltpu.make_async_copy(order_ref, order_buf, sem)
        order_copy.start()

        @pl.when(top)
        def _():
            g_buf[...] = cot_ref[at_rows, :]

        @pl.when(jnp.logical_not(top))
        def _():
            g_buf[...] = inc_ref[...]

        for k in range(8):
            parts = [dot(g_buf[:, col(8 * k + i)], w1_ref[8 * k + i]).astype(jnp.bfloat16) for i in range(8)]
            parts = exchange(parts, 1)
            for i in range(8):
                mid_buf[8 * i + k] = parts[i]
                right_ref[at_rows, col(F + 8 * k + i)] = g_buf[:, col(8 * k + i)]

        inner = jnp.zeros((rows, B), jnp.float32)
        for low in range(8):
            parts = exchange([mid_buf[8 * low + g] for g in range(8)], 4)
            for g in range(8):
                at = col(8 * g + low)
                gp = (parts[g].astype(jnp.float32) * slope_ref[at_rows, at]).astype(jnp.bfloat16)
                right_ref[at_rows, at] = gp
                gh = dot(gp, w0_ref[8 * g + low])
                gh_buf[:, at] = gh
                term = gh * xh_ref[at_rows, at]
                part = term[:8]
                for t in range(8, rows, 8):
                    part = part + term[t : t + 8]
                part_ref[:, at] = part_ref[:, at] + part
                inner = inner + term * gain_ref[:, at]

        inner = jnp.sum(inner, axis=1, keepdims=True) * (1.0 / (F * B))
        inv = inv_ref[at_rows, :]
        inner = inner * inv
        order_copy.wait()

        @pl.loop(0, F, unroll=8)
        def _(j):
            at = col(j)
            to = col(order_buf[j])
            value = g_buf[:, to].astype(jnp.float32) + (inv * gain_ref[:, at]) * gh_buf[:, at] - xh_ref[at_rows, at] * inner
            value = value.astype(jnp.bfloat16)
            send_ref[:, to] = value
            right_ref[at_rows, col(2 * F + j)] = value


def stage(step, segments, order, cot, inc, xh, inv, slope, gain, w1, w0, left, carried):
    n = xh.shape[0]
    rows = n // CHUNKS
    wide = F * B
    bf, f32 = jnp.bfloat16, jnp.float32
    first = carried is None
    args = [order, cot, inc, xh, inv, slope, gain, w1, w0, left] + ([] if first else list(carried))
    return pl.pallas_call(
        functools.partial(stage_kernel, step, segments, first),
        out_shape=(
            jax.ShapeDtypeStruct((rows, wide), bf),
            jax.ShapeDtypeStruct((n, 3 * wide), bf),
            jax.ShapeDtypeStruct((8, wide), f32),
        ),
        in_specs=[ANY] + [VMEM] * (9 if first else 11),
        out_specs=(VMEM,) * 3,
        scratch_shapes=[
            pltpu.VMEM((rows, wide), bf),
            pltpu.VMEM((F, rows, B), bf),
            pltpu.VMEM((rows, wide), f32),
            pltpu.SMEM((F,), jnp.int32),
            pltpu.SemaphoreType.DMA,
        ],
        input_output_aliases={} if first else {10: 1, 11: 2},
        compiler_params=pltpu.CompilerParams(vmem_limit_bytes=LIMIT),
        cost_estimate=pl.CostEstimate(flops=4 * rows * wide * B, bytes_accessed=6 << 20, transcendentals=0),
        name="stage",
    )(*args)


def product(scale, blocks, p, table_ref, perm_ref, column_ref, left_ref, right_ref):
    which = table_ref[perm_ref[p] ^ (lax.axis_index("dp") * blocks)]
    at = col(column_ref[which])
    return dot_tn(left_ref[:, at], right_ref[:, at]) * scale


def gain_row(part_ref, scale, j):
    return jnp.sum(part_ref[:, j * B : (j + 1) * B], axis=0, keepdims=True) * scale


def products(scale, blocks, jobs, unroll, *lookup):
    for start, count, target in jobs:

        @pl.loop(0, count, unroll=unroll)
        def _(p):
            value = product(scale, blocks, start + p, *lookup)
            target[pl.ds(pl.multiple_of(p * B, B), B), :] = value.astype(target.dtype)


def first_kernel(scale, blocks, table_ref, perm_ref, column_ref, left_ref, right_ref, part_ref, send_ref, gain_ref):
    count = F // 2
    for j in range(F):
        gain_ref[j : j + 1, :] = gain_row(part_ref, scale, j)
    send_ref[count * B :, :] = gain_ref[...].astype(jnp.bfloat16)
    products(scale, blocks, [(0, count, send_ref)], 8, table_ref, perm_ref, column_ref, left_ref, right_ref)


def second_kernel(scale, blocks, table_ref, perm_ref, column_ref, left_ref, right_ref, keep_ref, send_ref):
    count = F // 2
    jobs = [(F, count, keep_ref), (count, count, send_ref)]
    products(scale, blocks, jobs, 4, table_ref, perm_ref, column_ref, left_ref, right_ref)


def third_kernel(scale, blocks, table_ref, perm_ref, column_ref, left_ref, right_ref, after_ref, keep_ref, grad_ref, sem):
    count = F // 2
    out = pltpu.make_async_copy(right_ref.at[:, pl.ds(2 * F * B, F * B)], grad_ref, sem)
    out.start()
    products(scale, blocks, [(F + count, count, keep_ref)], 1, table_ref, perm_ref, column_ref, left_ref, right_ref)
    out.wait()


def call(kernel, name, args, specs, outs, out_specs, scratch=()):
    return pl.pallas_call(
        kernel,
        out_shape=outs,
        in_specs=specs,
        out_specs=out_specs,
        scratch_shapes=scratch,
        compiler_params=pltpu.CompilerParams(vmem_limit_bytes=LIMIT),
        cost_estimate=pl.CostEstimate(flops=1 << 26, bytes_accessed=4 << 20, transcendentals=0),
        name=name,
    )(*args)


def sum_rows(terms, start, size, target):
    piece = math.gcd(size, 256)

    @pl.loop(0, size // piece)
    def _(k):
        total = 0.0
        for ref, offset in terms:
            at = pl.ds(pl.multiple_of(offset + start + k * piece, piece), piece)
            total = total + ref[at, :].astype(jnp.float32)
        target(k, piece, total)


def into(ref, start=0):
    def write(k, piece, value):
        ref[pl.ds(pl.multiple_of(start + k * piece, piece), piece), :] = value.astype(ref.dtype)

    return write


def split_kernel(sizes, offsets, send_only, where, *refs):
    count = len(sizes)
    inputs, outs = refs[: len(where[0])], refs[len(where[0]) + 1 :]
    gain_ref = refs[len(where[0])]
    for side in range(count):
        terms = [(inputs[i], offsets[side][n]) for n, i in enumerate(where[1 + side])]
        half = sizes[side] if send_only else sizes[side] // 2
        sum_rows(terms, 0, half, into(outs[side]))
        if not send_only:
            sum_rows(terms, half, half, into(outs[count + side]))
    carrier = inputs[where[1][-1]]
    total = gain_ref[...] + carrier[carrier.shape[0] - F :, :].astype(jnp.float32)
    outs[-1][...] = total
    outs[0][outs[0].shape[0] - F :, :] = total.astype(jnp.bfloat16)


def gather(terms):
    arrays, where, offsets = [], [], []
    for side in terms:
        places = []
        for array, _ in side:
            found = [i for i, a in enumerate(arrays) if a is array]
            places.append(found[0] if found else len(arrays))
            if not found:
                arrays.append(array)
        where.append(places)
        offsets.append([offset for _, offset in side])
    return arrays, [list(range(len(arrays)))] + where, offsets


def split(terms, sizes, gain, send_only):
    arrays, where, offsets = gather(terms)
    f32 = jnp.float32
    halves = [size if send_only else size // 2 for size in sizes]
    outs = [jax.ShapeDtypeStruct((half + (F if side == 0 else 0), B), jnp.bfloat16) for side, half in enumerate(halves)]
    outs += [] if send_only else [jax.ShapeDtypeStruct((half, B), f32) for half in halves]
    outs += [jax.ShapeDtypeStruct((F, B), f32)]
    got = call(
        functools.partial(split_kernel, sizes, offsets, send_only, where),
        "split", (*arrays, gain), [VMEM] * (len(arrays) + 1), tuple(outs), (VMEM,) * len(outs),
    )
    count = len(sizes)
    return got[:count], got[count:-1], got[-1]


def last_kernel(sizes, offsets, where, dp, *refs):
    inputs, gain_ref = refs[: len(where[0])], refs[len(where[0])]
    out_ref, own_ref, gain_buf = refs[len(where[0]) + 1 :]
    start = 0
    for side, size in enumerate(sizes):
        terms = [(inputs[i], offsets[side][n]) for n, i in enumerate(where[1 + side])]
        sum_rows(terms, 0, size, into(out_ref, start))
        start += size
    carrier = inputs[where[1][-1]]
    gain_buf[...] = gain_ref[...] + carrier[carrier.shape[0] - F :, :].astype(jnp.float32)
    each = F // dp
    me = lax.axis_index("dp")
    for r in range(each):
        own_ref[:, r * B : (r + 1) * B] = gain_buf[pl.ds(me * each + r, 1), :]


def last(terms, sizes, dp, gain):
    arrays, where, offsets = gather(terms)
    f32 = jnp.float32
    return call(
        functools.partial(last_kernel, sizes, offsets, where, dp),
        "last", (*arrays, gain), [VMEM] * (len(arrays) + 1),
        (jax.ShapeDtypeStruct((sum(sizes), B), f32), jax.ShapeDtypeStruct((1, F * B // dp), f32)),
        (VMEM, VMEM), [pltpu.VMEM((F, B), f32)],
    )


def weight_gradients(scale, blocks, dp, tables, left, right, part):
    bf, f32 = jnp.bfloat16, jnp.float32
    n = left.shape[0]
    rows = F * B // 2
    bits = dp.bit_length() - 2
    cut = (dp // 4) * max(blocks // 2, 1) * B
    sizes = [cut, rows - cut]
    lookup = [SMEM] * 3 + [VMEM] * 2
    send, gain = call(
        functools.partial(first_kernel, scale, blocks), "first", (*tables, left, right, part), lookup + [VMEM],
        (jax.ShapeDtypeStruct((rows + F, B), bf), jax.ShapeDtypeStruct((F, B), f32)), (VMEM, VMEM),
    )
    got = swap(send, 0)
    keep, send = call(
        functools.partial(second_kernel, scale, blocks), "second", (*tables, left, right), lookup,
        (jax.ShapeDtypeStruct((rows, B), f32), jax.ShapeDtypeStruct((rows, B), bf)), (VMEM, VMEM),
    )
    got_rest = swap(send, 0)
    sends, _, gain = split([[(keep, 0), (got, 0)], [(keep, cut), (got, cut)]], sizes, gain, True)
    gots = [swap(sends[0], 1), swap(sends[1], bits)]
    keep, input_gradient = call(
        functools.partial(third_kernel, scale, blocks), "third", (*tables, left, right, gain), lookup + [VMEM],
        (jax.ShapeDtypeStruct((rows, B), f32), jax.ShapeDtypeStruct((n, F * B), bf)), (VMEM, ANY), [pltpu.SemaphoreType.DMA],
    )
    terms = [[(keep, at), (got_rest, at), (array, 0)] for at, array in zip((0, cut), gots)]
    for index in range(1, bits):
        sends, keeps, gain = split(terms, sizes, gain, False)
        sizes = [size // 2 for size in sizes]
        gots = [swap(sends[0], index + 1), swap(sends[1], bits - index)]
        terms = [[(kept, 0), (array, 0)] for kept, array in zip(keeps, gots)]
    owned, own_gain = last(terms, sizes, dp, gain)
    return owned, own_gain, input_gradient


def order_of(bits, low_first):
    def place(q):
        digits = [(q >> k) & 1 for k in range(bits)]
        if not low_first:
            digits = digits[::-1]
        return [1 - d for d in digits]

    return sorted(range(1 << bits), key=place)


def swap(array, bit):
    size = lax.axis_size("dp")
    return lax.ppermute(array, "dp", [(i, i ^ (1 << bit)) for i in range(size)])


def local(acts, weights, gains, cotangent, block_order, owner_table):
    x = acts[0]
    n = x.shape[0]
    segments = lax.axis_size("segment")
    dp = lax.axis_size("dp")
    blocks = 2 * F // dp
    scale = 1.0 / math.sqrt(n * dp)
    rows = n // CHUNKS
    steps = CHUNKS + LAG * (segments - 1)
    pairs = [(i, i - 1) for i in range(1, segments)]
    raw, w1, w0 = prepare(block_order, weights[0])
    cot = shuffle(block_order, cotangent)
    forward_plan, mix_plan = plans(segments)
    sent, carried, ahead = [], None, None
    for step in range(steps):
        if any(plan[step] for plan in forward_plan):
            ahead = forward(step, forward_plan, x, gains, raw, ahead)
        inv, left, z, slope, xh = ahead
        inc = sent[step - LAG] if step >= LAG else cot[:rows]
        out = stage(step, segments, block_order, cot, inc, xh, inv, slope, gains, w1, w0, left, carried)
        carried = out[1:]
        if step < steps - LAG:
            sent.append(lax.ppermute(out[0], "segment", pairs))
        if any(plan[step] for plan in mix_plan):
            ahead = (inv, mix(step, mix_plan, z, left), z, slope, xh)
    left = ahead[1]
    right, part = carried

    bits = dp.bit_length() - 2
    first = max(blocks // 2, 1)
    one = [(2 * q) * blocks + i for q in order_of(bits, True) for i in range(first)]
    two = [(2 * q) * blocks + i for q in order_of(bits, False) for i in range(first, blocks)]
    places = one[: len(one) // 2] + two[: len(two) // 2] + one[len(one) // 2 :] + two[len(two) // 2 :]
    perm = jnp.array([p + blocks for p in places] + places, jnp.int32)
    column = jnp.concatenate([jnp.arange(F, dtype=jnp.int32), F + block_order])
    owned, own_gain, input_gradient = weight_gradients(
        scale, blocks, dp, (owner_table, perm, column), left, right, part
    )
    return input_gradient[None], owned.reshape(1, blocks, B, B), own_gain


def solution(mesh):
    return jax.shard_map(
        local,
        mesh=mesh,
        in_specs=(
            P("segment", "dp", None),
            P("segment", None, None, None, None),
            P("segment", None),
            P("dp", None),
            P(),
            P(),
        ),
        out_specs=(P("segment", "dp", None), P("segment", "dp", None, None), P("segment", "dp")),
        check_vma=False,
    )
```

```python
import functools
import math

import jax
import jax.numpy as jnp
from jax import lax
from jax.experimental import pallas as pl
from jax.experimental.pallas import tpu as pltpu
from jax.sharding import PartitionSpec as P

F = 64
B = 128
EPS = 1e-05
CHUNKS = 8
LAG = 2
AHEAD = 1
PREPARE_LIMIT = 46 << 20
ANY = pl.BlockSpec(memory_space=pl.ANY)
VMEM = pl.BlockSpec(memory_space=pltpu.VMEM)
HBM = pl.BlockSpec(memory_space=pltpu.HBM)
SMEM = pl.BlockSpec(memory_space=pltpu.SMEM)
TN = (((0,), (0,)), ((), ()))
LIMIT = 16 << 20


def dot(a, b):
    return jnp.dot(a, b, preferred_element_type=jnp.float32)


def dot_tn(a, b):
    return lax.dot_general(a, b, TN, preferred_element_type=jnp.float32)


def col(j):
    if isinstance(j, int):
        return pl.ds(j * B, B)
    return pl.ds(pl.multiple_of(j * B, B), B)


def exchange(parts, lane_bit):
    lane = lax.broadcasted_iota(jnp.int32, parts[0].shape, 1)
    parts = list(parts)
    for i in range(3):
        shift = 1 << (lane_bit + i)
        upper = (lane & shift) != 0
        for low in range(8):
            if low & (1 << i):
                continue
            high = low | (1 << i)
            a, b = parts[low], parts[high]
            parts[low] = jnp.where(upper, pltpu.roll(b, shift, 1), a)
            parts[high] = jnp.where(upper, b, pltpu.roll(a, B - shift, 1))
    return parts


def gelu_pair(v):
    cdf = 0.5 * (1.0 + lax.erf(v * 0.7071067811865476))
    density = jnp.exp(-0.5 * v * v) * 0.3989422804014327
    return v * cdf, cdf + v * density


def matrix(rule):
    row = lax.broadcasted_iota(jnp.int32, (B, B), 0)
    column = lax.broadcasted_iota(jnp.int32, (B, B), 1)
    return rule(row, column).astype(jnp.float32).astype(jnp.bfloat16)


def prepare_kernel(order_ref, w_ref, raw_ref, w1_ref, w0_ref, w_buf, sem):
    half = B // 2
    part = F // 4
    spans = [pl.ds(k * part, part) for k in range(4)]
    seconds = [pltpu.make_async_copy(w_ref.at[1, at], w_buf.at[at], sem.at[k]) for k, at in enumerate(spans)]
    firsts = [pltpu.make_async_copy(w_ref.at[0, at], raw_ref.at[at], sem.at[4 + k]) for k, at in enumerate(spans)]
    for copy in seconds + firsts:
        copy.start()
    mixed = matrix(lambda r, c: c == 2 * (r % half) + r // half)
    eye = matrix(lambda r, c: c == r)
    for k in range(4):
        seconds[k].wait()
        for j in range(k * part, (k + 1) * part):
            w1_ref[order_ref[j]] = dot_tn(w_buf[j], mixed).astype(jnp.bfloat16)
    for k in range(4):
        firsts[k].wait()
        for j in range(k * part, (k + 1) * part):
            w0_ref[j] = dot_tn(raw_ref[j], eye).astype(jnp.bfloat16)


def prepare(order, weights):
    bf = jnp.bfloat16
    factor = jax.ShapeDtypeStruct((F, B, B), bf)
    return pl.pallas_call(
        prepare_kernel,
        out_shape=(factor, factor, factor),
        in_specs=[SMEM, HBM],
        out_specs=(VMEM,) * 3,
        scratch_shapes=[pltpu.VMEM((F, B, B), bf), pltpu.SemaphoreType.DMA((8,))],
        compiler_params=pltpu.CompilerParams(vmem_limit_bytes=PREPARE_LIMIT),
        name="prepare",
    )(order, weights)


def shuffle_kernel(order_ref, cot_ref, out_ref):
    @pl.loop(0, F, unroll=4)
    def _(j):
        out_ref[:, col(order_ref[j])] = cot_ref[:, col(j)]


def shuffle(order, cotangent):
    return pl.pallas_call(
        shuffle_kernel,
        out_shape=jax.ShapeDtypeStruct(cotangent.shape, cotangent.dtype),
        in_specs=[SMEM, VMEM],
        out_specs=VMEM,
        compiler_params=pltpu.CompilerParams(vmem_limit_bytes=LIMIT),
        name="shuffle",
    )(order, cotangent)


def span(plan, step, ahead=0):
    position = lax.axis_index("segment")
    first = last = 0
    for p, pieces in enumerate(plan):
        first = jnp.where(position == p, sum(pieces[:step]), first)
        last = jnp.where(position == p, sum(pieces[: step + 1]), last)
    if ahead:
        total = sum(plan[-1])
        more = jnp.where(jnp.logical_and(position == len(plan) - 1, lax.axis_index("dp") % 2 == 1), ahead, 0)
        first = jnp.minimum(first + (more if step else 0), total)
        last = jnp.minimum(last + more, total)
    return first, last


def plans(segments):
    steps = CHUNKS + LAG * (segments - 1)
    forward_plan, mix_plan = [], []
    for p in range(segments):
        begin = LAG * (segments - 1 - p)
        ahead, blend = [0] * steps, [0] * steps
        if begin == 0:
            ahead[:CHUNKS] = [1] * CHUNKS
        elif begin < 4:
            ahead[:4] = [3, 3, 1, 1]
        else:
            ahead[:3] = [3, 3, 2]
        if begin >= 6:
            blend[3:5] = [2, 2]
        else:
            blend[steps - LAG - 1] = CHUNKS // 2
        forward_plan.append(ahead)
        mix_plan.append(blend)
    return forward_plan, mix_plan


def forward_kernel(step, plan, first, *refs):
    x_ref, gain_ref, w_ref = refs[:3]
    inv_ref, left_ref, z_ref, slope_ref, xh_ref, pre_buf = refs[3:] if first else refs[8:]
    rows = pre_buf.shape[0]

    @pl.loop(*span(plan, step, AHEAD))
    def _(chunk):
        at_rows = pl.ds(pl.multiple_of(chunk * rows, rows), rows)

        def square(j, total):
            v = x_ref[at_rows, col(j)].astype(jnp.float32)
            return total + v * v

        total = lax.fori_loop(0, F, square, jnp.zeros((rows, B), jnp.float32), unroll=8)
        mean = jnp.sum(total, axis=1, keepdims=True) * (1.0 / (F * B))
        inv = jnp.broadcast_to(lax.rsqrt(mean + EPS), (rows, B))
        inv_ref[at_rows, :] = inv

        @pl.loop(0, F, unroll=32)
        def _(j):
            xh = x_ref[at_rows, col(j)].astype(jnp.float32) * inv
            xh_ref[at_rows, col(j)] = xh
            h = (xh * gain_ref[:, col(j)]).astype(jnp.bfloat16)
            left_ref[at_rows, col(j)] = h
            pre_buf[:, col(j)] = dot(h, w_ref[j])

        @pl.loop(0, F, unroll=8)
        def _(j):
            z, slope = gelu_pair(pre_buf[:, col(j)])
            slope_ref[at_rows, col(j)] = slope
            z_ref[at_rows, col(j)] = z.astype(jnp.bfloat16)


def forward(step, plan, x, gain, w0, carried):
    n = x.shape[0]
    wide = F * B
    first = carried is None
    return pl.pallas_call(
        functools.partial(forward_kernel, step, plan, first),
        out_shape=(
            jax.ShapeDtypeStruct((n, B), jnp.float32),
            jax.ShapeDtypeStruct((n, 2 * wide), jnp.bfloat16),
            jax.ShapeDtypeStruct((n, wide), jnp.bfloat16),
            jax.ShapeDtypeStruct((n, wide), jnp.float32),
            jax.ShapeDtypeStruct((n, wide), jnp.float32),
        ),
        in_specs=[VMEM] * (3 if first else 8),
        out_specs=(VMEM,) * 5,
        scratch_shapes=[pltpu.VMEM((n // CHUNKS, wide), jnp.float32)],
        input_output_aliases={} if first else {3: 0, 4: 1, 5: 2, 6: 3, 7: 4},
        compiler_params=pltpu.CompilerParams(vmem_limit_bytes=LIMIT),
        cost_estimate=pl.CostEstimate(flops=1 << 20, bytes_accessed=4 << 20, transcendentals=0),
        name="forward",
    )(x, gain, w0, *(() if first else carried))


def mix_kernel(step, plan, z_ref, old_ref, left_ref, low_buf, mid_buf):
    rows = low_buf.shape[1]
    half = B // 2
    apart = matrix(lambda r, c: c == r // 2 + half * (r % 2))

    @pl.loop(*span(plan, step))
    def _(pair):
        at_rows = pl.ds(pl.multiple_of(pair * rows, rows), rows)

        @pl.loop(0, F, unroll=32)
        def _(j):
            low_buf[j] = dot(z_ref[at_rows, col(j)], apart).astype(jnp.bfloat16)

        @pl.loop(0, 8, unroll=4)
        def _(k):
            parts = exchange([low_buf[8 * k + i] for i in range(8)], 0)
            for i in range(8):
                mid_buf[8 * i + k] = parts[i]

        @pl.loop(0, 8, unroll=4)
        def _(low):
            parts = exchange([mid_buf[8 * low + g] for g in range(8)], 3)
            for g in range(8):
                left_ref[at_rows, col(F + 8 * g + low)] = parts[g]


def mix(step, plan, z, left):
    n = z.shape[0]
    return pl.pallas_call(
        functools.partial(mix_kernel, step, plan),
        out_shape=jax.ShapeDtypeStruct((n, 2 * F * B), jnp.bfloat16),
        in_specs=[VMEM] * 2,
        out_specs=VMEM,
        scratch_shapes=[pltpu.VMEM((F, 2 * n // CHUNKS, B), jnp.bfloat16)] * 2,
        input_output_aliases={1: 0},
        compiler_params=pltpu.CompilerParams(vmem_limit_bytes=LIMIT),
        cost_estimate=pl.CostEstimate(flops=1 << 20, bytes_accessed=4 << 20, transcendentals=0),
        name="mix",
    )(z, left)


def stage_kernel(step, segments, first, *refs):
    (order_ref, cot_ref, inc_ref, xh_ref, inv_ref, slope_ref, gain_ref, w1_ref, w0_ref) = refs[:9]
    refs = refs[10:] if first else refs[12:]
    (send_ref, right_ref, part_ref, g_buf, mid_buf, gh_buf, order_buf, sem) = refs
    rows = g_buf.shape[0]
    wide = F * B
    position = lax.axis_index("segment")
    chunk = step - LAG * (segments - 1 - position)
    top = position == segments - 1
    if first:
        part_ref[...] = jnp.zeros_like(part_ref)

    @pl.when(jnp.logical_and(chunk >= 0, chunk < CHUNKS))
    def _():
        at_rows = pl.ds(pl.multiple_of(chunk * rows, rows), rows)
        order_copy = pltpu.make_async_copy(order_ref, order_buf, sem)
        order_copy.start()

        @pl.when(top)
        def _():
            g_buf[...] = cot_ref[at_rows, :]

        @pl.when(jnp.logical_not(top))
        def _():
            g_buf[...] = inc_ref[...]

        for k in range(8):
            parts = [dot(g_buf[:, col(8 * k + i)], w1_ref[8 * k + i]).astype(jnp.bfloat16) for i in range(8)]
            parts = exchange(parts, 1)
            for i in range(8):
                mid_buf[8 * i + k] = parts[i]
                right_ref[at_rows, col(F + 8 * k + i)] = g_buf[:, col(8 * k + i)]

        inner = jnp.zeros((rows, B), jnp.float32)
        for low in range(8):
            parts = exchange([mid_buf[8 * low + g] for g in range(8)], 4)
            for g in range(8):
                at = col(8 * g + low)
                gp = (parts[g].astype(jnp.float32) * slope_ref[at_rows, at]).astype(jnp.bfloat16)
                right_ref[at_rows, at] = gp
                gh = dot(gp, w0_ref[8 * g + low])
                gh_buf[:, at] = gh
                term = gh * xh_ref[at_rows, at]
                part = term[:8]
                for t in range(8, rows, 8):
                    part = part + term[t : t + 8]
                part_ref[:, at] = part_ref[:, at] + part
                inner = inner + term * gain_ref[:, at]

        inner = jnp.sum(inner, axis=1, keepdims=True) * (1.0 / (F * B))
        inv = inv_ref[at_rows, :]
        inner = inner * inv
        order_copy.wait()

        @pl.loop(0, F, unroll=8)
        def _(j):
            at = col(j)
            to = col(order_buf[j])
            value = g_buf[:, to].astype(jnp.float32) + (inv * gain_ref[:, at]) * gh_buf[:, at] - xh_ref[at_rows, at] * inner
            value = value.astype(jnp.bfloat16)
            send_ref[:, to] = value
            right_ref[at_rows, col(2 * F + j)] = value


def stage(step, segments, order, cot, inc, xh, inv, slope, gain, w1, w0, left, carried):
    n = xh.shape[0]
    rows = n // CHUNKS
    wide = F * B
    bf, f32 = jnp.bfloat16, jnp.float32
    first = carried is None
    args = [order, cot, inc, xh, inv, slope, gain, w1, w0, left] + ([] if first else list(carried))
    return pl.pallas_call(
        functools.partial(stage_kernel, step, segments, first),
        out_shape=(
            jax.ShapeDtypeStruct((rows, wide), bf),
            jax.ShapeDtypeStruct((n, 3 * wide), bf),
            jax.ShapeDtypeStruct((8, wide), f32),
        ),
        in_specs=[ANY] + [VMEM] * (9 if first else 11),
        out_specs=(VMEM,) * 3,
        scratch_shapes=[
            pltpu.VMEM((rows, wide), bf),
            pltpu.VMEM((F, rows, B), bf),
            pltpu.VMEM((rows, wide), f32),
            pltpu.SMEM((F,), jnp.int32),
            pltpu.SemaphoreType.DMA,
        ],
        input_output_aliases={} if first else {10: 1, 11: 2},
        compiler_params=pltpu.CompilerParams(vmem_limit_bytes=LIMIT),
        cost_estimate=pl.CostEstimate(flops=4 * rows * wide * B, bytes_accessed=6 << 20, transcendentals=0),
        name="stage",
    )(*args)


def product(scale, blocks, p, table_ref, perm_ref, column_ref, left_ref, right_ref):
    which = table_ref[perm_ref[p] ^ (lax.axis_index("dp") * blocks)]
    at = col(column_ref[which])
    return dot_tn(left_ref[:, at], right_ref[:, at]) * scale


def gain_row(part_ref, scale, j):
    return jnp.sum(part_ref[:, j * B : (j + 1) * B], axis=0, keepdims=True) * scale


def products(scale, blocks, jobs, unroll, *lookup):
    for start, count, target in jobs:

        @pl.loop(0, count, unroll=unroll)
        def _(p):
            value = product(scale, blocks, start + p, *lookup)
            target[pl.ds(pl.multiple_of(p * B, B), B), :] = value.astype(target.dtype)


def first_kernel(scale, blocks, table_ref, perm_ref, column_ref, left_ref, right_ref, part_ref, send_ref, gain_ref):
    count = F // 2
    for j in range(F):
        gain_ref[j : j + 1, :] = gain_row(part_ref, scale, j)
    send_ref[count * B :, :] = gain_ref[...].astype(jnp.bfloat16)
    products(scale, blocks, [(0, count, send_ref)], 8, table_ref, perm_ref, column_ref, left_ref, right_ref)


def second_kernel(scale, blocks, table_ref, perm_ref, column_ref, left_ref, right_ref, keep_ref, send_ref):
    count = F // 2
    jobs = [(F, count, keep_ref), (count, count, send_ref)]
    products(scale, blocks, jobs, 8, table_ref, perm_ref, column_ref, left_ref, right_ref)


def third_kernel(scale, blocks, table_ref, perm_ref, column_ref, left_ref, right_ref, after_ref, keep_ref, grad_ref, sem):
    count = F // 2
    out = pltpu.make_async_copy(right_ref.at[:, pl.ds(2 * F * B, F * B)], grad_ref, sem)
    out.start()
    products(scale, blocks, [(F + count, count, keep_ref)], 2, table_ref, perm_ref, column_ref, left_ref, right_ref)
    out.wait()


def call(kernel, name, args, specs, outs, out_specs, scratch=()):
    return pl.pallas_call(
        kernel,
        out_shape=outs,
        in_specs=specs,
        out_specs=out_specs,
        scratch_shapes=scratch,
        compiler_params=pltpu.CompilerParams(vmem_limit_bytes=LIMIT),
        cost_estimate=pl.CostEstimate(flops=1 << 26, bytes_accessed=4 << 20, transcendentals=0),
        name=name,
    )(*args)


def sum_rows(terms, start, size, target):
    piece = math.gcd(size, 256)

    @pl.loop(0, size // piece)
    def _(k):
        total = 0.0
        for ref, offset in terms:
            at = pl.ds(pl.multiple_of(offset + start + k * piece, piece), piece)
            total = total + ref[at, :].astype(jnp.float32)
        target(k, piece, total)


def into(ref, start=0):
    def write(k, piece, value):
        ref[pl.ds(pl.multiple_of(start + k * piece, piece), piece), :] = value.astype(ref.dtype)

    return write


def split_kernel(sizes, offsets, send_only, where, *refs):
    count = len(sizes)
    inputs, outs = refs[: len(where[0])], refs[len(where[0]) + 1 :]
    gain_ref = refs[len(where[0])]
    for side in range(count):
        terms = [(inputs[i], offsets[side][n]) for n, i in enumerate(where[1 + side])]
        half = sizes[side] if send_only else sizes[side] // 2
        sum_rows(terms, 0, half, into(outs[side]))
        if not send_only:
            sum_rows(terms, half, half, into(outs[count + side]))
    carrier = inputs[where[1][-1]]
    total = gain_ref[...] + carrier[carrier.shape[0] - F :, :].astype(jnp.float32)
    outs[-1][...] = total
    outs[0][outs[0].shape[0] - F :, :] = total.astype(jnp.bfloat16)


def gather(terms):
    arrays, where, offsets = [], [], []
    for side in terms:
        places = []
        for array, _ in side:
            found = [i for i, a in enumerate(arrays) if a is array]
            places.append(found[0] if found else len(arrays))
            if not found:
                arrays.append(array)
        where.append(places)
        offsets.append([offset for _, offset in side])
    return arrays, [list(range(len(arrays)))] + where, offsets


def split(terms, sizes, gain, send_only):
    arrays, where, offsets = gather(terms)
    f32 = jnp.float32
    halves = [size if send_only else size // 2 for size in sizes]
    outs = [jax.ShapeDtypeStruct((half + (F if side == 0 else 0), B), jnp.bfloat16) for side, half in enumerate(halves)]
    outs += [] if send_only else [jax.ShapeDtypeStruct((half, B), f32) for half in halves]
    outs += [jax.ShapeDtypeStruct((F, B), f32)]
    got = call(
        functools.partial(split_kernel, sizes, offsets, send_only, where),
        "split", (*arrays, gain), [VMEM] * (len(arrays) + 1), tuple(outs), (VMEM,) * len(outs),
    )
    count = len(sizes)
    return got[:count], got[count:-1], got[-1]


def last_kernel(sizes, offsets, where, dp, *refs):
    inputs, gain_ref = refs[: len(where[0])], refs[len(where[0])]
    out_ref, own_ref, gain_buf = refs[len(where[0]) + 1 :]
    start = 0
    for side, size in enumerate(sizes):
        terms = [(inputs[i], offsets[side][n]) for n, i in enumerate(where[1 + side])]
        sum_rows(terms, 0, size, into(out_ref, start))
        start += size
    carrier = inputs[where[1][-1]]
    gain_buf[...] = gain_ref[...] + carrier[carrier.shape[0] - F :, :].astype(jnp.float32)
    each = F // dp
    me = lax.axis_index("dp")
    for r in range(each):
        own_ref[:, r * B : (r + 1) * B] = gain_buf[pl.ds(me * each + r, 1), :]


def last(terms, sizes, dp, gain):
    arrays, where, offsets = gather(terms)
    f32 = jnp.float32
    return call(
        functools.partial(last_kernel, sizes, offsets, where, dp),
        "last", (*arrays, gain), [VMEM] * (len(arrays) + 1),
        (jax.ShapeDtypeStruct((sum(sizes), B), f32), jax.ShapeDtypeStruct((1, F * B // dp), f32)),
        (VMEM, VMEM), [pltpu.VMEM((F, B), f32)],
    )


def weight_gradients(scale, blocks, dp, tables, left, right, part):
    bf, f32 = jnp.bfloat16, jnp.float32
    n = left.shape[0]
    rows = F * B // 2
    bits = dp.bit_length() - 2
    cut = (dp // 4) * max(blocks // 2, 1) * B
    sizes = [cut, rows - cut]
    lookup = [SMEM] * 3 + [VMEM] * 2
    send, gain = call(
        functools.partial(first_kernel, scale, blocks), "first", (*tables, left, right, part), lookup + [VMEM],
        (jax.ShapeDtypeStruct((rows + F, B), bf), jax.ShapeDtypeStruct((F, B), f32)), (VMEM, VMEM),
    )
    got = swap(send, 0)
    keep, send = call(
        functools.partial(second_kernel, scale, blocks), "second", (*tables, left, right), lookup,
        (jax.ShapeDtypeStruct((rows, B), f32), jax.ShapeDtypeStruct((rows, B), bf)), (VMEM, VMEM),
    )
    got_rest = swap(send, 0)
    sends, _, gain = split([[(keep, 0), (got, 0)], [(keep, cut), (got, cut)]], sizes, gain, True)
    gots = [swap(sends[0], 1), swap(sends[1], bits)]
    keep, input_gradient = call(
        functools.partial(third_kernel, scale, blocks), "third", (*tables, left, right, gain), lookup + [VMEM],
        (jax.ShapeDtypeStruct((rows, B), f32), jax.ShapeDtypeStruct((n, F * B), bf)), (VMEM, ANY), [pltpu.SemaphoreType.DMA],
    )
    terms = [[(keep, at), (got_rest, at), (array, 0)] for at, array in zip((0, cut), gots)]
    for index in range(1, bits):
        sends, keeps, gain = split(terms, sizes, gain, False)
        sizes = [size // 2 for size in sizes]
        gots = [swap(sends[0], index + 1), swap(sends[1], bits - index)]
        terms = [[(kept, 0), (array, 0)] for kept, array in zip(keeps, gots)]
    owned, own_gain = last(terms, sizes, dp, gain)
    return owned, own_gain, input_gradient


def order_of(bits, low_first):
    def place(q):
        digits = [(q >> k) & 1 for k in range(bits)]
        if not low_first:
            digits = digits[::-1]
        return [1 - d for d in digits]

    return sorted(range(1 << bits), key=place)


def swap(array, bit):
    size = lax.axis_size("dp")
    return lax.ppermute(array, "dp", [(i, i ^ (1 << bit)) for i in range(size)])


def local(acts, weights, gains, cotangent, block_order, owner_table):
    x = acts[0]
    n = x.shape[0]
    segments = lax.axis_size("segment")
    dp = lax.axis_size("dp")
    blocks = 2 * F // dp
    scale = 1.0 / math.sqrt(n * dp)
    rows = n // CHUNKS
    steps = CHUNKS + LAG * (segments - 1)
    pairs = [(i, i - 1) for i in range(1, segments)]
    raw, w1, w0 = prepare(block_order, weights[0])
    cot = shuffle(block_order, cotangent)
    forward_plan, mix_plan = plans(segments)
    sent, carried, ahead = [], None, None
    for step in range(steps):
        if any(plan[step] for plan in forward_plan):
            ahead = forward(step, forward_plan, x, gains, raw, ahead)
        inv, left, z, slope, xh = ahead
        inc = sent[step - LAG] if step >= LAG else cot[:rows]
        out = stage(step, segments, block_order, cot, inc, xh, inv, slope, gains, w1, w0, left, carried)
        carried = out[1:]
        if step < steps - LAG:
            sent.append(lax.ppermute(out[0], "segment", pairs))
        if any(plan[step] for plan in mix_plan):
            ahead = (inv, mix(step, mix_plan, z, left), z, slope, xh)
    left = ahead[1]
    right, part = carried

    bits = dp.bit_length() - 2
    first = max(blocks // 2, 1)
    one = [(2 * q) * blocks + i for q in order_of(bits, True) for i in range(first)]
    two = [(2 * q) * blocks + i for q in order_of(bits, False) for i in range(first, blocks)]
    places = one[: len(one) // 2] + two[: len(two) // 2] + one[len(one) // 2 :] + two[len(two) // 2 :]
    perm = jnp.array([p + blocks for p in places] + places, jnp.int32)
    column = jnp.concatenate([jnp.arange(F, dtype=jnp.int32), F + block_order])
    owned, own_gain, input_gradient = weight_gradients(
        scale, blocks, dp, (owner_table, perm, column), left, right, part
    )
    return input_gradient[None], owned.reshape(1, blocks, B, B), own_gain


def solution(mesh):
    return jax.shard_map(
        local,
        mesh=mesh,
        in_specs=(
            P("segment", "dp", None),
            P("segment", None, None, None, None),
            P("segment", None),
            P("dp", None),
            P(),
            P(),
        ),
        out_specs=(P("segment", "dp", None), P("segment", "dp", None, None), P("segment", "dp")),
        check_vma=False,
    )
```
